32 devices in a mesh: sec: 4 (over x, core), row: 4 (over z), col: 2 (over y).
Axes of the slice: x: 2, y: 2, z: 4, core: 2. Of those that a mesh axis runs over, the one named last changes fastest.
Arguments:
- images: float32 [4, 1024, 512], P('sec', 'row', 'col'), may hold values from -6 to 6
- stiffness: float32 [4, 1024, 512], P('sec', 'row', 'col'), may hold values from 0.1 to 1
Outputs:
- tensor: float32 [5, 4, 1024, 512], P(None, 'sec', 'row', 'col')
- field: float32 [2, 4, 1024, 512], P(None, 'sec', 'row', 'col')
The draws below stay inside these ranges and needn't reach their ends.
All inputs are finite; a program needn't handle non-finite values.
Results may differ from the reference program's by a relative error of at most 0.00002.
Values sent between devices are 32-bit elements; how exact they have to be, the bound alone decides.
A program may use at most 64 MiB of HBM per device.

```python
import math
import jax
import jax.numpy as jnp

RADIUS = 4
SWEEPS = 4
ROUNDS = 2
SECTIONS = 4
HEIGHT = 1024
WIDTH = 512


def steps_of(rng, extent, pieces, least, high):
    def one(position, blocks):
        heights = jax.random.uniform(jax.random.fold_in(jax.random.fold_in(rng, 6), position), (blocks,), jnp.float32, least / len(pieces), high / len(pieces))
        return jnp.repeat(jnp.exp(heights), extent[position] // blocks).reshape((-1,) + (1,) * (len(extent) - position - 1))

    factor_of = one(*pieces[0])
    for cut in pieces[1:]:
        factor_of = factor_of * one(*cut)
    return factor_of


def scatter_about(key, shape, width, reach, cuts=(), held_as=jnp.bfloat16):
    array = width * jax.random.normal(key, shape, jnp.float32)
    if cuts:
        array = array * steps_of(key, shape, cuts, -0.22, 0.18)
    return jnp.clip(array, -reach, reach).astype(held_as)


def setup_inputs(seed: int = 0) -> dict:
    seeds = jax.random.split(jax.random.key(seed), 3)
    return {
        "images": scatter_about(seeds[0], (SECTIONS, HEIGHT, WIDTH), 1.0, 6.0, ((0, 4), (1, 4), (2, 2)), jnp.float32),
        "stiffness": jnp.clip(jnp.exp(math.log(1.0) - 2.3025851 * jax.random.uniform(seeds[1], (SECTIONS, HEIGHT, WIDTH), jnp.float32) ** steps_of(seeds[1], (SECTIONS, HEIGHT, WIDTH), ((0, 4), (1, 4), (2, 2)), -0.2, 0.2)), 0.1, 1.0),
    }


coupling = 0.25

def gradients(padded):
    grad_y = (padded[..., 2:, 1:-1] - padded[..., :-2, 1:-1]) * 0.5
    grad_x = (padded[..., 1:-1, 2:] - padded[..., 1:-1, :-2]) * 0.5
    return (grad_y, grad_x)

def products(grad_y, grad_x, change):
    return jnp.stack([grad_x * grad_x, grad_x * grad_y, grad_y * grad_y, grad_x * change, grad_y * change])

def window_mean(widened, radius):
    row_count = widened.shape[-2] - 2 * radius
    col_count = widened.shape[-1] - 2 * radius
    partial_rows = widened[..., 0:row_count, :]
    for offset in range(1, 2 * radius + 1):
        partial_rows = partial_rows + widened[..., offset:offset + row_count, :]
    summed = partial_rows[..., 0:col_count]
    for offset in range(1, 2 * radius + 1):
        summed = summed + partial_rows[..., offset:offset + col_count]
    return summed / float((2 * radius + 1) ** 2)

def couplings(stiff_pad):
    centre = stiff_pad[..., 1:-1, 1:-1]
    kappa_up = jnp.sqrt(centre * stiff_pad[..., :-2, 1:-1])
    kappa_down = jnp.sqrt(centre * stiff_pad[..., 2:, 1:-1])
    kappa_left = jnp.sqrt(centre * stiff_pad[..., 1:-1, :-2])
    kappa_right = jnp.sqrt(centre * stiff_pad[..., 1:-1, 2:])
    kappa_sum = kappa_up + kappa_down + kappa_left + kappa_right
    return ((kappa_up, kappa_down, kappa_left, kappa_right), kappa_sum)

def jacobi(field_pad, kappas, kappa_sum, tensor, beside):
    neighbour = kappas[0] * field_pad[..., :-2, 1:-1] + kappas[1] * field_pad[..., 2:, 1:-1]
    neighbour = neighbour + kappas[2] * field_pad[..., 1:-1, :-2] + kappas[3] * field_pad[..., 1:-1, 2:]
    diagonal = kappa_sum + 2.0 * coupling
    first_diag = tensor[0] + diagonal
    second_diag = tensor[2] + diagonal
    off_diag = tensor[1]
    determinant = first_diag * second_diag - off_diag * off_diag
    right_x = coupling * beside[0] + neighbour[0] - tensor[3]
    right_y = coupling * beside[1] + neighbour[1] - tensor[4]
    new_x = (second_diag * right_x - off_diag * right_y) / determinant
    new_y = (first_diag * right_y - off_diag * right_x) / determinant
    return jnp.stack([new_x, new_y])

def reference(images, stiffness):
    section_count = images.shape[0]
    later = jnp.concatenate([images[1:], jnp.zeros_like(images[:1])], axis=0)
    padded = jnp.pad(images, ((0, 0), (1, 1), (1, 1)))
    grad_y, grad_x = gradients(padded)
    stacked = products(grad_y, grad_x, later - images)
    widened = jnp.pad(stacked, ((0, 0), (0, 0), (RADIUS, RADIUS), (RADIUS, RADIUS)))
    tensor = window_mean(widened, RADIUS)
    keep = (jnp.arange(section_count) < section_count - 1).astype(tensor.dtype)
    tensor = tensor * keep[None, :, None, None]
    stiff_pad = jnp.pad(stiffness, ((0, 0), (1, 1), (1, 1)))
    kappas, kappa_sum = couplings(stiff_pad)
    field = jnp.zeros((2,) + images.shape, images.dtype)
    for round_index in range(ROUNDS):
        if round_index == 0:
            beside = jnp.zeros_like(field)
        else:
            below_part = jnp.concatenate([jnp.zeros_like(field[:, :1]), field[:, :-1]], axis=1)
            above_part = jnp.concatenate([field[:, 1:], jnp.zeros_like(field[:, :1])], axis=1)
            beside = below_part + above_part
        for sweep_index in range(SWEEPS):
            field_pad = jnp.pad(field, ((0, 0), (0, 0), (1, 1), (1, 1)))
            field = jacobi(field_pad, kappas, kappa_sum, tensor, beside)
    return (tensor, field)
```

```python
import functools

import jax
import jax.numpy as jnp
from jax import lax
from jax.experimental import pallas as pl
from jax.experimental.pallas import tpu as pltpu
from jax.sharding import PartitionSpec as P

RADIUS = 4
SWEEPS = 4
ROUNDS = 2
COUPLING = 0.25
MESH = pl.DeviceIdType.MESH

LANES = 128
HALO = 16
EDGE = HALO + 8
GRAD = 16
WIN = 64
SWEEP = 32
SLOT = 16
CHUNK = 64
FOLD = LANES // (2 * SLOT)

(
    TILE_B, ROW_A_UP, ROW_A_DOWN, ROW_S_UP, ROW_S_DOWN, FWD_TOP, FWD_BOTTOM, COL_RIGHT, COL_LEFT,
    FWD_RIGHT, FWD_LEFT,
) = range(11)
KINDS = 11


def lane_roll(x, shift):
    return pltpu.roll(x, shift % x.shape[1], 1)


def columns_of(k):
    return slice(k * LANES, (k + 1) * LANES)


def shifted(blocks, shift, lane):
    rolled = [lane_roll(x, shift) for x in blocks]
    out = []
    for k, here in enumerate(rolled):
        if shift > 0:
            out.append(jnp.where(lane < shift, rolled[k - 1], here))
        else:
            out.append(jnp.where(lane >= LANES + shift, rolled[(k + 1) % len(rolled)], here))
    return out


def add(*terms):
    return [sum(xs[1:], xs[0]) for xs in zip(*terms)]


def kernel(
    counts, images, stiff, tensor_out, field_out,
    a, b, s, q, rq, gx, gy, pr, p3, tt, ca, cb, cc, g0, g1, g2, g3, g4, kk, field,
    send_right, send_left, got_left, got_right, next_left, next_right,
    rim, rim_before, rim_after, main_before, main_after, band,
    local_sem, send_sem, recv_sem, chunk_send, chunk_recv,
):
    sec, row, col = (lax.axis_index(name) for name in ("sec", "row", "col"))
    n_sec, n_row, n_col = counts
    rows, width = images.shape[1], images.shape[2]
    nb, total, _ = a.shape
    nw = nb - 1
    has_prev, has_next = sec > 0, sec < n_sec - 1
    has_up, has_down = row > 0, row < n_row - 1
    has_left, has_right = col > 0, col < n_col - 1
    sides = (
        (has_prev, (sec - 1, row, col)), (has_next, (sec + 1, row, col)),
        (has_up, (sec, row - 1, col)), (has_down, (sec, row + 1, col)),
        (has_left, (sec, row, col - 1)), (has_right, (sec, row, col + 1)),
    )
    prev_id, next_id, up_id, down_id, left_id, right_id = (side[1] for side in sides)
    end = EDGE + rows
    first, last = EDGE - HALO, end + HALO
    inner = pl.ds(EDGE, rows)
    main = pl.ds(0, nw)
    top, bottom = pl.ds(EDGE - HALO, HALO), pl.ds(end, HALO)
    piece = (last - first) // FOLD

    def remote(src, dst, k, device, part=0):
        return pltpu.make_async_remote_copy(
            src_ref=src, dst_ref=dst, send_sem=send_sem.at[k, part],
            recv_sem=recv_sem.at[k, part], device_id=device, device_id_type=MESH,
        )

    def columns(k):
        return pl.ds(k * LANES, LANES)

    loads = [
        pltpu.make_async_copy(src.at[0, :, columns(k)], dst.at[k, inner], local_sem.at[i, k])
        for i, (src, dst) in enumerate(((images, a), (stiff, s)))
        for k in range(nw)
    ]
    for copy in loads:
        copy.start()
    barrier = pltpu.get_barrier_semaphore()
    for there, device in sides:
        @pl.when(there)
        def _():
            pl.semaphore_signal(barrier, inc=1, device_id=device, device_id_type=MESH)

    def clear(ref):
        ref[...] = jnp.zeros(ref.shape, jnp.float32)

    @pl.when(jnp.logical_not(has_up))
    def _():
        clear(a.at[main, top])
        clear(s.at[main, top])

    @pl.when(jnp.logical_not(has_down))
    def _():
        clear(a.at[main, bottom])
        clear(s.at[main, bottom])

    @pl.when(jnp.logical_not(has_left))
    def _():
        clear(got_left)

    @pl.when(jnp.logical_not(has_right))
    def _():
        clear(got_right)

    @pl.when(jnp.logical_not(has_next))
    def _():
        clear(b)
        clear(next_left)
        clear(next_right)
        clear(rim_after)
        clear(main_after)

    @pl.when(jnp.logical_not(has_prev))
    def _():
        clear(rim_before)
        clear(main_before)

    pl.semaphore_wait(barrier, sum(jnp.where(there, 1, 0) for there, _device in sides))

    def by_block(src, at, dst, to, k, device):
        return [
            remote(src.at[0, at, columns(p)], dst.at[p, to], k, device, p) for p in range(nw)
        ]

    low, high = pl.ds(0, HALO), pl.ds(rows - HALO, HALO)
    tile_b = by_block(images, pl.ds(0, rows), b, inner, TILE_B, prev_id)
    up = by_block(stiff, low, s, bottom, ROW_S_UP, up_id)
    up += by_block(images, low, a, bottom, ROW_A_UP, up_id)
    down = by_block(stiff, high, s, top, ROW_S_DOWN, down_id)
    down += by_block(images, high, a, top, ROW_A_DOWN, down_id)
    col_right = remote(send_right, got_left, COL_RIGHT, right_id)
    col_left = remote(send_left, got_right, COL_LEFT, left_id)
    forward_rows = [
        remote(a.at[main, top], b.at[main, top], FWD_TOP, prev_id),
        remote(a.at[main, bottom], b.at[main, bottom], FWD_BOTTOM, prev_id),
    ]
    forward_cols = [
        remote(got_left, next_left, FWD_LEFT, prev_id),
        remote(got_right, next_right, FWD_RIGHT, prev_id),
    ]

    def when_start(there, copies):
        @pl.when(there)
        def _():
            for copy in copies:
                copy.start()

    def when_got(there, copies):
        @pl.when(there)
        def _():
            for copy in copies:
                copy.wait_recv()

    def when_sent(there, copies):
        @pl.when(there)
        def _():
            for copy in copies:
                copy.wait_send()

    when_start(has_up, up)
    when_start(has_down, down)
    when_start(has_prev, tile_b)
    for copy in loads:
        copy.wait()
    when_got(has_up, down)
    when_got(has_down, up)
    when_start(has_prev, forward_rows)

    def lanes_of(count):
        return lax.broadcasted_iota(jnp.int32, (count, LANES), 1)

    lane = lanes_of(piece)

    def packed(block, at):
        out = jnp.zeros((piece, LANES), jnp.float32)
        for j in range(FOLD):
            span = pl.ds(first + j * piece, piece)
            for k, ref in enumerate((a, s)):
                low = (2 * j + k) * SLOT
                moved = lane_roll(ref[block, span, :], low - at)
                out = jnp.where((lane >= low) & (lane < low + SLOT), moved, out)
        return out

    def unpack(ref, left, right, k):
        for j in range(FOLD):
            low = (2 * j + k) * SLOT
            from_right = jnp.where(lane < SLOT, lane_roll(right[...], -low), 0.0)
            from_left = lane_roll(left[...], LANES - SLOT - low)
            ref[nw, pl.ds(first + j * piece, piece), :] = jnp.where(
                lane >= LANES - SLOT, from_left, from_right
            )

    @pl.when(has_right)
    def _():
        send_right[...] = packed(nw - 1, LANES - SLOT)
        col_right.start()

    @pl.when(has_left)
    def _():
        send_left[...] = packed(0, 0)
        col_left.start()

    when_got(has_left, [col_right])
    when_got(has_right, [col_left])
    when_start(has_prev, forward_cols)
    unpack(a, got_left, got_right, 0)
    unpack(s, got_left, got_right, 1)

    def get(ref, r, step, *lead):
        return [ref[(*lead, k, pl.ds(r, step), slice(None))] for k in range(nb)]

    def put(ref, values, r, step, *lead):
        for k, value in enumerate(values):
            ref[(*lead, k, pl.ds(r, step), slice(None))] = value

    def blocks(low, high, step, body):
        for r in range(low, high, step):
            body(r, min(step, high - r))

    def gradient(r, step):
        lane = lanes_of(step)
        rim_ok = ((lane < LANES // 2) & has_right) | ((lane >= LANES // 2) & has_left)
        mid = get(a, r, step)
        after, before = shifted(mid, -1, lane), shifted(mid, 1, lane)
        under, over = get(a, r + 1, step), get(a, r - 1, step)
        dx = [x - y for x, y in zip(after, before)]
        dy = [x - y for x, y in zip(under, over)]
        dx[nw], dy[nw] = jnp.where(rim_ok, dx[nw], 0.0), jnp.where(rim_ok, dy[nw], 0.0)
        put(gx, dx, r, step)
        put(gy, dy, r, step)
        put(pr, [x * x for x in dx], r, step, 0)
        put(pr, [x * y for x, y in zip(dx, dy)], r, step, 1)
        put(pr, [y * y for y in dy], r, step, 2)
        stiff_here = get(s, r, step)
        inverse = [lax.rsqrt(jnp.maximum(x, 0.05)) for x in stiff_here]
        put(rq, inverse, r, step)
        put(q, [x * y for x, y in zip(stiff_here, inverse)], r, step)

    blocks(first, last, GRAD, gradient)

    for there, at in ((has_up, top), (has_down, bottom)):
        @pl.when(jnp.logical_not(there))
        def _():
            for ref in (gx, gy):
                clear(ref.at[:, at])
            clear(pr.at[pl.ds(0, 3), :, at])

    def three_rows(ks):
        def body(r, step):
            for k in ks:
                put(p3, add(*(get(pr, r + d, step, k) for d in (-1, 0, 1))), r, step, k)

        return body

    kept = jnp.where(has_next, jnp.float32(1.0), jnp.float32(0.0))
    cells = float((2 * RADIUS + 1) ** 2)

    src = lax.broadcasted_iota(jnp.int32, (nb * LANES, nb * LANES), 0)
    dst = lax.broadcasted_iota(jnp.int32, (nb * LANES, nb * LANES), 1)
    fold_at = nw * LANES + LANES // 2
    src = jnp.where(src < fold_at, src, src - nb * LANES)
    dst = jnp.where(dst < fold_at, dst, dst - nb * LANES)
    band[...] = jnp.where(jnp.abs(src - dst) <= RADIUS, 1.0, 0.0).astype(jnp.bfloat16)

    def window(ks, factor):
        scale = kept * (factor / cells)

        def body(r, step):
            for k in ks:
                x = jnp.concatenate(add(*(get(p3, r + d, step, k) for d in (-3, 0, 3))), axis=1)
                coarse = x.astype(jnp.bfloat16)
                fine = (x - coarse.astype(jnp.float32)).astype(jnp.bfloat16)
                both = jnp.concatenate([coarse, fine], axis=0)
                y = jnp.dot(both, band[...], preferred_element_type=jnp.float32)
                y = (y[:step] + y[step:]) * scale
                value = [y[:, columns_of(j)] for j in range(nb)]
                put(tt, value, r, step, k)
                if EDGE <= r < end:
                    for j in range(nw):
                        tensor_out[k, 0, pl.ds(r - EDGE, step), columns(j)] = value[j]

        body(first, 16)
        blocks(EDGE, end, WIN, body)
        body(end, 16)

    blocks(first, last, 16, three_rows((0, 1, 2)))
    window((0, 1, 2), 0.25)

    when_got(has_next, tile_b + forward_rows + forward_cols)
    unpack(b, next_left, next_right, 0)

    def change(r, step):
        moved = [x - y for x, y in zip(get(b, r, step), get(a, r, step))]
        put(pr, [x * y for x, y in zip(get(gx, r, step), moved)], r, step, 3)
        put(pr, [x * y for x, y in zip(get(gy, r, step), moved)], r, step, 4)

    blocks(first, last, 32, change)
    blocks(first, last, 16, three_rows((3, 4)))
    window((3, 4), 0.5)

    def near(source, r, step, part, count):
        mid = get(source, r, step, part)
        lane = lanes_of(step)
        return add(
            get(source, r - 1, step, part), get(source, r + 1, step, part),
            shifted(mid, 1, lane), shifted(mid, -1, lane),
        )[:count]

    def relaxed(source, r, step, start, count):
        nx, ny = (near(source, r, step, part, count) for part in range(2))
        xx, xy, yy = (get(ref, r, step)[:count] for ref in (ca, cb, cc))
        x, y = start
        return (
            [x[k] + (xx[k] * nx[k] - xy[k] * ny[k]) for k in range(count)],
            [y[k] + (yy[k] * ny[k] - xy[k] * nx[k]) for k in range(count)],
        )

    def setup(r, step):
        lane = lanes_of(step)
        xx, xy, yy, xt, yt = (get(tt, r, step, k) for k in range(5))
        mid = get(q, r, step)
        around = add(
            get(q, r - 1, step), get(q, r + 1, step), shifted(mid, 1, lane), shifted(mid, -1, lane)
        )
        at = pl.ds(r, step)
        for k in range(nb):
            diag = mid[k] * around[k] + 2.0 * COUPLING
            one, two = xx[k] + diag, yy[k] + diag
            inverse = mid[k] / (one * two - xy[k] * xy[k])
            xa, xb, xc = two * inverse, xy[k] * inverse, one * inverse
            g0[0, k, at, :] = xb * yt[k] - xa * xt[k]
            g0[1, k, at, :] = xb * xt[k] - xc * yt[k]
            for ref, value in ((ca, xa), (cb, xb), (cc, xc)):
                ref[k, at, :] = value * mid[k]

    def sweep(source, start, target, unscaled=None):
        def body(r, step):
            new = relaxed(
                source, r, step, [get(start, r, step, part) for part in range(2)], nb
            )
            here = get(rq, r, step) if unscaled is not None else None
            for part in range(2):
                if target is not None:
                    put(target, new[part], r, step, part)
                if unscaled is not None:
                    put(unscaled, [x * y for x, y in zip(new[part], here)], r, step, part)

        return body

    bounds = list(range(first, last - CHUNK + 1, CHUNK)) + [last]
    chunks = len(bounds) - 1

    def stages(c, bodies, lead, ends):
        for k, body in enumerate(bodies):
            ahead = 8 * (lead - k)
            margin = ends[k == len(bodies) - 1]
            low = first + margin if c == 0 else bounds[c] + ahead
            high = last - margin if c == chunks - 1 else bounds[c + 1] + ahead
            blocks(low, high, SWEEP, body)

    first_round = [setup, sweep(g0, g0, g1), sweep(g1, g0, g2), sweep(g2, g0, g3, field)]

    to_next, to_prev = [], []
    for c in range(chunks):
        stages(c, first_round, SWEEPS - 1, (8, 8))
        low, high = bounds[c], bounds[c + 1]
        folded = pl.ds((low - first) // FOLD, (high - low) // FOLD)
        pack_rim(field, rim, low, high, first, nw)
        rows_sent = pl.ds(max(low, first + 8), min(high, last - 8) - max(low, first + 8))

        def moves(rims, mains, device, way):
            pairs = (
                (rim.at[folded], rims.at[folded]),
                (field.at[:, main, rows_sent], mains.at[:, main, rows_sent]),
            )
            return [
                pltpu.make_async_remote_copy(
                    src_ref=src, dst_ref=dst, send_sem=chunk_send.at[way + i, c],
                    recv_sem=chunk_recv.at[way + i, c], device_id=device, device_id_type=MESH,
                )
                for i, (src, dst) in enumerate(pairs)
            ]

        to_next.append(moves(rim_before, main_before, next_id, 0))
        to_prev.append(moves(rim_after, main_after, prev_id, 2))
        when_start(has_next, to_next[c])
        when_start(has_prev, to_prev[c])

    def coupled(r, step):
        at = pl.ds(r, step)

        def beside(part, ref):
            return [
                main_before[part, k, at, :] + main_after[part, k, at, :] for k in range(nw)
            ] + [ref[nw, at, :]]

        x, y = beside(0, gx), beside(1, gy)
        xx, xy, yy = (get(ref, r, step) for ref in (ca, cb, cc))
        weight = [v * COUPLING for v in get(rq, r, step)]
        old = [get(g0, r, step, part) for part in range(2)]
        start = (
            [old[0][k] + weight[k] * (xx[k] * x[k] - xy[k] * y[k]) for k in range(nb)],
            [old[1][k] + weight[k] * (yy[k] * y[k] - xy[k] * x[k]) for k in range(nb)],
        )
        new = relaxed(g3, r, step, start, nb)
        for part in range(2):
            put(kk, start[part], r, step, part)
            put(g1, new[part], r, step, part)

    def final(r, step):
        start = [get(kk, r, step, part) for part in range(2)]
        new = relaxed(g4, r, step, start, nw)
        here = get(rq, r, step)
        for part in range(2):
            for k in range(nw):
                field_out[part, 0, pl.ds(r - EDGE, step), columns(k)] = new[part][k] * here[k]

    second_round = [coupled, sweep(g1, kk, g2), sweep(g2, kk, g4), final]
    for c in range(chunks):
        when_got(has_prev, to_next[c])
        when_got(has_next, to_prev[c])
        low, high = bounds[c], bounds[c + 1]
        size = (high - low) // FOLD
        folded = pl.ds((low - first) // FOLD, size)
        both = rim_before[folded, :] + rim_after[folded, :]
        lane = lanes_of(size)
        for j in range(FOLD):
            for k, ref in enumerate((gx, gy)):
                slot = (2 * j + k) * SLOT
                head = jnp.where(lane < 8, lane_roll(both, -slot), 0.0)
                tail = lane_roll(both, LANES - 16 - slot)
                ref[nw, pl.ds(low + j * size, size), :] = jnp.where(
                    lane >= LANES - 8, tail, head
                )
        stages(c, second_round, 0, (8, 16))

    for c in range(chunks):
        when_sent(has_next, to_next[c])
        when_sent(has_prev, to_prev[c])
    when_sent(has_up, up)
    when_sent(has_down, down)
    when_sent(has_right, [col_right])
    when_sent(has_left, [col_left])
    when_sent(has_prev, tile_b + forward_rows + forward_cols)


def pack_rim(field, rim, low, high, first, nw):
    size = (high - low) // FOLD
    lane = lax.broadcasted_iota(jnp.int32, (size, LANES), 1)
    out = jnp.zeros((size, LANES), jnp.float32)
    for j in range(FOLD):
        at = pl.ds(low + j * size, size)
        for k in range(2):
            slot = (2 * j + k) * SLOT
            block = field[k, nw, at, :]
            head, tail = lane_roll(block, slot), lane_roll(block, slot + SLOT)
            out = jnp.where((lane >= slot) & (lane < slot + 8), head, out)
            out = jnp.where((lane >= slot + 8) & (lane < slot + 16), tail, out)
    rim[pl.ds((low - first) // FOLD, size), :] = out


def local(counts, images, stiffness):
    _, rows, width = images.shape
    nw = width // LANES
    nb = nw + 1
    total = rows + 2 * EDGE
    f32 = jnp.float32
    plane = pltpu.VMEM((nb, total, LANES), f32)
    five = pltpu.VMEM((5, nb, total, LANES), f32)
    pair = pltpu.VMEM((2, nb, total, LANES), f32)
    packet = pltpu.VMEM(((rows + 2 * HALO) // FOLD, LANES), f32)
    mains = pltpu.VMEM((2, nw, total, LANES), f32)
    chunks = (rows + 2 * HALO) // CHUNK
    return pl.pallas_call(
        functools.partial(kernel, counts),
        out_shape=(
            jax.ShapeDtypeStruct((5, 1, rows, width), f32),
            jax.ShapeDtypeStruct((2, 1, rows, width), f32),
        ),
        in_specs=[pl.BlockSpec(memory_space=pltpu.HBM)] * 2,
        out_specs=[pl.BlockSpec(memory_space=pltpu.VMEM)] * 2,
        scratch_shapes=[plane] * 7
        + [five] * 3
        + [plane] * 3
        + [pair] * 7
        + [packet] * 9
        + [mains] * 2
        + [pltpu.VMEM((nb * LANES, nb * LANES), jnp.bfloat16)]
        + [
            pltpu.SemaphoreType.DMA((2, nw)),
            pltpu.SemaphoreType.DMA((KINDS, nw)),
            pltpu.SemaphoreType.DMA((KINDS, nw)),
            pltpu.SemaphoreType.DMA((4, chunks)),
            pltpu.SemaphoreType.DMA((4, chunks)),
        ],
        compiler_params=pltpu.CompilerParams(
            collective_id=0, has_side_effects=True, vmem_limit_bytes=48 * 1024 * 1024
        ),
    )(*(pltpu.with_memory_space_constraint(x, pltpu.HBM) for x in (images, stiffness)))


def solution(mesh):
    counts = tuple(mesh.shape[name] for name in ("sec", "row", "col"))
    spec = P("sec", "row", "col")
    out = P(None, "sec", "row", "col")
    return jax.shard_map(
        functools.partial(local, counts), mesh=mesh, in_specs=(spec, spec),
        out_specs=(out, out), check_vma=False,
    )
```

```python
import functools

import jax
import jax.numpy as jnp
from jax import lax
from jax.experimental import pallas as pl
from jax.experimental.pallas import tpu as pltpu
from jax.sharding import PartitionSpec as P

RADIUS = 4
SWEEPS = 4
ROUNDS = 2
COUPLING = 0.25
MESH = pl.DeviceIdType.MESH

LANES = 128
HALO = 16
EDGE = HALO + 8
GRAD = 16
WIN = 64
SWEEP = 32
EARLY = 2
SLOT = 16
CHUNK = 64
FOLD = LANES // (2 * SLOT)

(
    TILE_B, ROW_A_UP, ROW_A_DOWN, ROW_S_UP, ROW_S_DOWN, FWD_TOP, FWD_BOTTOM, COL_RIGHT, COL_LEFT,
    FWD_RIGHT, FWD_LEFT,
) = range(11)
KINDS = 11


def lane_roll(x, shift):
    return pltpu.roll(x, shift % x.shape[1], 1)


def columns_of(k):
    return slice(k * LANES, (k + 1) * LANES)


def shifted(blocks, shift, lane):
    rolled = [lane_roll(x, shift) for x in blocks]
    out = []
    for k, here in enumerate(rolled):
        if shift > 0:
            out.append(jnp.where(lane < shift, rolled[k - 1], here))
        else:
            out.append(jnp.where(lane >= LANES + shift, rolled[(k + 1) % len(rolled)], here))
    return out


def add(*terms):
    return [sum(xs[1:], xs[0]) for xs in zip(*terms)]


def kernel(
    counts, images, stiff, tensor_out, field_out,
    a, b, s, q, rq, gx, gy, pr, p3, tt, ca, cb, cc, g0, g1, g2, g3, g4, kk, field,
    send_right, send_left, got_left, got_right, next_left, next_right,
    rim, rim_before, rim_after, main_before, main_after, band,
    local_sem, send_sem, recv_sem, chunk_send, chunk_recv, tile_send, tile_recv,
):
    sec, row, col = (lax.axis_index(name) for name in ("sec", "row", "col"))
    n_sec, n_row, n_col = counts
    rows, width = images.shape[1], images.shape[2]
    nb, total, _ = a.shape
    nw = nb - 1
    has_prev, has_next = sec > 0, sec < n_sec - 1
    has_up, has_down = row > 0, row < n_row - 1
    has_left, has_right = col > 0, col < n_col - 1
    sides = (
        (has_prev, (sec - 1, row, col)), (has_next, (sec + 1, row, col)),
        (has_up, (sec, row - 1, col)), (has_down, (sec, row + 1, col)),
        (has_left, (sec, row, col - 1)), (has_right, (sec, row, col + 1)),
    )
    prev_id, next_id, up_id, down_id, left_id, right_id = (side[1] for side in sides)
    end = EDGE + rows
    first, last = EDGE - HALO, end + HALO
    inner = pl.ds(EDGE, rows)
    main = pl.ds(0, nw)
    top, bottom = pl.ds(EDGE - HALO, HALO), pl.ds(end, HALO)
    piece = (last - first) // FOLD

    def remote(src, dst, k, device, part=0):
        return pltpu.make_async_remote_copy(
            src_ref=src, dst_ref=dst, send_sem=send_sem.at[k, part],
            recv_sem=recv_sem.at[k, part], device_id=device, device_id_type=MESH,
        )

    def columns(k):
        return pl.ds(k * LANES, LANES)

    loads = [
        pltpu.make_async_copy(src.at[0, :, columns(k)], dst.at[k, inner], local_sem.at[i, k])
        for i, (src, dst) in enumerate(((images, a), (stiff, s)))
        for k in range(nw)
    ]
    for copy in loads:
        copy.start()
    barrier = pltpu.get_barrier_semaphore()
    for there, device in sides:
        @pl.when(there)
        def _():
            pl.semaphore_signal(barrier, inc=1, device_id=device, device_id_type=MESH)

    def clear(ref):
        ref[...] = jnp.zeros(ref.shape, jnp.float32)

    @pl.when(jnp.logical_not(has_up))
    def _():
        clear(a.at[main, top])
        clear(s.at[main, top])

    @pl.when(jnp.logical_not(has_down))
    def _():
        clear(a.at[main, bottom])
        clear(s.at[main, bottom])

    @pl.when(jnp.logical_not(has_left))
    def _():
        clear(got_left)

    @pl.when(jnp.logical_not(has_right))
    def _():
        clear(got_right)

    @pl.when(jnp.logical_not(has_next))
    def _():
        clear(b)
        clear(next_left)
        clear(next_right)
        clear(rim_after)
        clear(main_after)

    @pl.when(jnp.logical_not(has_prev))
    def _():
        clear(rim_before)
        clear(main_before)

    pl.semaphore_wait(barrier, sum(jnp.where(there, 1, 0) for there, _device in sides))

    def by_block(src, at, dst, to, k, device):
        return [
            remote(src.at[0, at, columns(p)], dst.at[p, to], k, device, p) for p in range(nw)
        ]

    low, high = pl.ds(0, HALO), pl.ds(rows - HALO, HALO)
    bounds = list(range(first, last - CHUNK + 1, CHUNK)) + [last]
    chunks = len(bounds) - 1
    ahead = 8 * (SWEEPS + 1)
    cuts = [0] + [min(high + ahead - EDGE, rows) for high in bounds[1:-1]] + [rows]

    def tile_piece(c):
        at, to = pl.ds(cuts[c], cuts[c + 1] - cuts[c]), pl.ds(EDGE + cuts[c], cuts[c + 1] - cuts[c])
        return [
            pltpu.make_async_remote_copy(
                src_ref=images.at[0, at, columns(p)], dst_ref=b.at[p, to],
                send_sem=tile_send.at[c, p], recv_sem=tile_recv.at[c, p],
                device_id=prev_id, device_id_type=MESH,
            )
            for p in range(nw)
        ]

    tile_b = [tile_piece(c) for c in range(chunks)]
    up = by_block(stiff, low, s, bottom, ROW_S_UP, up_id)
    up += by_block(images, low, a, bottom, ROW_A_UP, up_id)
    down = by_block(stiff, high, s, top, ROW_S_DOWN, down_id)
    down += by_block(images, high, a, top, ROW_A_DOWN, down_id)
    col_right = remote(send_right, got_left, COL_RIGHT, right_id)
    col_left = remote(send_left, got_right, COL_LEFT, left_id)
    forward_rows = [
        remote(a.at[main, top], b.at[main, top], FWD_TOP, prev_id),
        remote(a.at[main, bottom], b.at[main, bottom], FWD_BOTTOM, prev_id),
    ]
    forward_cols = [
        remote(got_left, next_left, FWD_LEFT, prev_id),
        remote(got_right, next_right, FWD_RIGHT, prev_id),
    ]

    def when_start(there, copies):
        @pl.when(there)
        def _():
            for copy in copies:
                copy.start()

    def when_got(there, copies):
        @pl.when(there)
        def _():
            for copy in copies:
                copy.wait_recv()

    def when_sent(there, copies):
        @pl.when(there)
        def _():
            for copy in copies:
                copy.wait_send()

    when_start(has_up, up)
    when_start(has_down, down)
    when_start(has_prev, sum(tile_b[:EARLY], []))
    for copy in loads:
        copy.wait()
    when_got(has_up, down)
    when_got(has_down, up)
    when_start(has_prev, forward_rows + sum(tile_b[EARLY:EARLY + 1], []))

    def lanes_of(count):
        return lax.broadcasted_iota(jnp.int32, (count, LANES), 1)

    lane = lanes_of(piece)

    def packed(block, at):
        out = jnp.zeros((piece, LANES), jnp.float32)
        for j in range(FOLD):
            span = pl.ds(first + j * piece, piece)
            for k, ref in enumerate((a, s)):
                low = (2 * j + k) * SLOT
                moved = lane_roll(ref[block, span, :], low - at)
                out = jnp.where((lane >= low) & (lane < low + SLOT), moved, out)
        return out

    def unpack(ref, left, right, k):
        for j in range(FOLD):
            low = (2 * j + k) * SLOT
            from_right = jnp.where(lane < SLOT, lane_roll(right[...], -low), 0.0)
            from_left = lane_roll(left[...], LANES - SLOT - low)
            ref[nw, pl.ds(first + j * piece, piece), :] = jnp.where(
                lane >= LANES - SLOT, from_left, from_right
            )

    @pl.when(has_right)
    def _():
        send_right[...] = packed(nw - 1, LANES - SLOT)
        col_right.start()

    @pl.when(has_left)
    def _():
        send_left[...] = packed(0, 0)
        col_left.start()

    when_got(has_left, [col_right])
    when_got(has_right, [col_left])
    when_start(has_prev, forward_cols + sum(tile_b[EARLY + 1:], []))
    unpack(a, got_left, got_right, 0)
    unpack(s, got_left, got_right, 1)

    def get(ref, r, step, *lead):
        return [ref[(*lead, k, pl.ds(r, step), slice(None))] for k in range(nb)]

    def put(ref, values, r, step, *lead):
        for k, value in enumerate(values):
            ref[(*lead, k, pl.ds(r, step), slice(None))] = value

    def blocks(low, high, step, body):
        for r in range(low, high, step):
            body(r, min(step, high - r))

    def gradient(r, step):
        lane = lanes_of(step)
        rim_ok = ((lane < LANES // 2) & has_right) | ((lane >= LANES // 2) & has_left)
        mid = get(a, r, step)
        after, before = shifted(mid, -1, lane), shifted(mid, 1, lane)
        under, over = get(a, r + 1, step), get(a, r - 1, step)
        dx = [x - y for x, y in zip(after, before)]
        dy = [x - y for x, y in zip(under, over)]
        dx[nw], dy[nw] = jnp.where(rim_ok, dx[nw], 0.0), jnp.where(rim_ok, dy[nw], 0.0)
        put(gx, dx, r, step)
        put(gy, dy, r, step)
        put(pr, [x * x for x in dx], r, step, 0)
        put(pr, [x * y for x, y in zip(dx, dy)], r, step, 1)
        put(pr, [y * y for y in dy], r, step, 2)
        stiff_here = get(s, r, step)
        inverse = [lax.rsqrt(jnp.maximum(x, 0.05)) for x in stiff_here]
        put(rq, inverse, r, step)
        put(q, [x * y for x, y in zip(stiff_here, inverse)], r, step)

    blocks(first, last, GRAD, gradient)

    for there, at in ((has_up, top), (has_down, bottom)):
        @pl.when(jnp.logical_not(there))
        def _():
            for ref in (gx, gy):
                clear(ref.at[:, at])
            clear(pr.at[pl.ds(0, 3), :, at])

    def three_rows(ks):
        def body(r, step):
            for k in ks:
                put(p3, add(*(get(pr, r + d, step, k) for d in (-1, 0, 1))), r, step, k)

        return body

    kept = jnp.where(has_next, jnp.float32(1.0), jnp.float32(0.0))
    cells = float((2 * RADIUS + 1) ** 2)

    src = lax.broadcasted_iota(jnp.int32, (nb * LANES, nb * LANES), 0)
    dst = lax.broadcasted_iota(jnp.int32, (nb * LANES, nb * LANES), 1)
    fold_at = nw * LANES + LANES // 2
    src = jnp.where(src < fold_at, src, src - nb * LANES)
    dst = jnp.where(dst < fold_at, dst, dst - nb * LANES)
    band[...] = jnp.where(jnp.abs(src - dst) <= RADIUS, 1.0, 0.0).astype(jnp.bfloat16)

    def window(low, high, ks, factor):
        scale = kept * (factor / cells)

        def body(r, step):
            for k in ks:
                x = jnp.concatenate(add(*(get(p3, r + d, step, k) for d in (-3, 0, 3))), axis=1)
                coarse = x.astype(jnp.bfloat16)
                fine = (x - coarse.astype(jnp.float32)).astype(jnp.bfloat16)
                both = jnp.concatenate([coarse, fine], axis=0)
                y = jnp.dot(both, band[...], preferred_element_type=jnp.float32)
                y = (y[:step] + y[step:]) * scale
                value = [y[:, columns_of(j)] for j in range(nb)]
                put(tt, value, r, step, k)
                if EDGE <= r < end:
                    for j in range(nw):
                        tensor_out[k, 0, pl.ds(r - EDGE, step), columns(j)] = value[j]

        if low < EDGE:
            body(low, EDGE - low)
        blocks(max(low, EDGE), min(high, end), WIN, body)
        if high > end:
            body(end, high - end)

    blocks(first, last, 16, three_rows((0, 1, 2)))
    window(first + 8, last - 8, (0, 1, 2), 0.25)


    def change(r, step):
        moved = [x - y for x, y in zip(get(b, r, step), get(a, r, step))]
        put(pr, [x * y for x, y in zip(get(gx, r, step), moved)], r, step, 3)
        put(pr, [x * y for x, y in zip(get(gy, r, step), moved)], r, step, 4)

    def near(source, r, step, part, count):
        mid = get(source, r, step, part)
        lane = lanes_of(step)
        return add(
            get(source, r - 1, step, part), get(source, r + 1, step, part),
            shifted(mid, 1, lane), shifted(mid, -1, lane),
        )[:count]

    def relaxed(source, r, step, start, count):
        nx, ny = (near(source, r, step, part, count) for part in range(2))
        xx, xy, yy = (get(ref, r, step)[:count] for ref in (ca, cb, cc))
        x, y = start
        return (
            [x[k] + (xx[k] * nx[k] - xy[k] * ny[k]) for k in range(count)],
            [y[k] + (yy[k] * ny[k] - xy[k] * nx[k]) for k in range(count)],
        )

    def setup(r, step):
        lane = lanes_of(step)
        xx, xy, yy, xt, yt = (get(tt, r, step, k) for k in range(5))
        mid = get(q, r, step)
        around = add(
            get(q, r - 1, step), get(q, r + 1, step), shifted(mid, 1, lane), shifted(mid, -1, lane)
        )
        at = pl.ds(r, step)
        for k in range(nb):
            diag = mid[k] * around[k] + 2.0 * COUPLING
            one, two = xx[k] + diag, yy[k] + diag
            inverse = mid[k] / (one * two - xy[k] * xy[k])
            xa, xb, xc = two * inverse, xy[k] * inverse, one * inverse
            g0[0, k, at, :] = xb * yt[k] - xa * xt[k]
            g0[1, k, at, :] = xb * xt[k] - xc * yt[k]
            for ref, value in ((ca, xa), (cb, xb), (cc, xc)):
                ref[k, at, :] = value * mid[k]

    def sweep(source, start, target, unscaled=None):
        def body(r, step):
            new = relaxed(
                source, r, step, [get(start, r, step, part) for part in range(2)], nb
            )
            here = get(rq, r, step) if unscaled is not None else None
            for part in range(2):
                if target is not None:
                    put(target, new[part], r, step, part)
                if unscaled is not None:
                    put(unscaled, [x * y for x, y in zip(new[part], here)], r, step, part)

        return body

    def span(c, ahead, margin):
        low = first + margin if c == 0 else bounds[c] + ahead
        high = last - margin if c == chunks - 1 else bounds[c + 1] + ahead
        return low, high

    def stages(c, bodies, lead, ends):
        for k, body in enumerate(bodies):
            blocks(*span(c, 8 * (lead - k), ends[k == len(bodies) - 1]), SWEEP, body)

    first_round = [setup, sweep(g0, g0, g1), sweep(g1, g0, g2), sweep(g2, g0, g3, field)]

    to_next, to_prev = [], []
    for c in range(chunks):
        when_got(has_next, tile_b[c])
        if c == 0:
            when_got(has_next, forward_rows + forward_cols)
            unpack(b, next_left, next_right, 0)
        settled = 8 * (SWEEPS - 1)
        blocks(*span(c, settled + 16, 0), 32, change)
        blocks(*span(c, settled + 8, 0), 16, three_rows((3, 4)))
        window(*span(c, settled, 8), (3, 4), 0.5)
        stages(c, first_round, SWEEPS - 1, (8, 8))
        low, high = bounds[c], bounds[c + 1]
        folded = pl.ds((low - first) // FOLD, (high - low) // FOLD)
        pack_rim(field, rim, low, high, first, nw)
        rows_sent = pl.ds(max(low, first + 8), min(high, last - 8) - max(low, first + 8))

        def moves(rims, mains, device, way):
            pairs = (
                (rim.at[folded], rims.at[folded]),
                (field.at[:, main, rows_sent], mains.at[:, main, rows_sent]),
            )
            return [
                pltpu.make_async_remote_copy(
                    src_ref=src, dst_ref=dst, send_sem=chunk_send.at[way + i, c],
                    recv_sem=chunk_recv.at[way + i, c], device_id=device, device_id_type=MESH,
                )
                for i, (src, dst) in enumerate(pairs)
            ]

        to_next.append(moves(rim_before, main_before, next_id, 0))
        to_prev.append(moves(rim_after, main_after, prev_id, 2))
        when_start(has_next, to_next[c])
        when_start(has_prev, to_prev[c])

    def coupled(r, step):
        at = pl.ds(r, step)

        def beside(part, ref):
            return [
                main_before[part, k, at, :] + main_after[part, k, at, :] for k in range(nw)
            ] + [ref[nw, at, :]]

        x, y = beside(0, gx), beside(1, gy)
        xx, xy, yy = (get(ref, r, step) for ref in (ca, cb, cc))
        weight = [v * COUPLING for v in get(rq, r, step)]
        old = [get(g0, r, step, part) for part in range(2)]
        start = (
            [old[0][k] + weight[k] * (xx[k] * x[k] - xy[k] * y[k]) for k in range(nb)],
            [old[1][k] + weight[k] * (yy[k] * y[k] - xy[k] * x[k]) for k in range(nb)],
        )
        new = relaxed(g3, r, step, start, nb)
        for part in range(2):
            put(kk, start[part], r, step, part)
            put(g1, new[part], r, step, part)

    def final(r, step):
        start = [get(kk, r, step, part) for part in range(2)]
        new = relaxed(g4, r, step, start, nw)
        here = get(rq, r, step)
        for part in range(2):
            for k in range(nw):
                field_out[part, 0, pl.ds(r - EDGE, step), columns(k)] = new[part][k] * here[k]

    second_round = [coupled, sweep(g1, kk, g2), sweep(g2, kk, g4), final]
    for c in range(chunks):
        when_got(has_prev, to_next[c])
        when_got(has_next, to_prev[c])
        low, high = bounds[c], bounds[c + 1]
        size = (high - low) // FOLD
        folded = pl.ds((low - first) // FOLD, size)
        both = rim_before[folded, :] + rim_after[folded, :]
        lane = lanes_of(size)
        for j in range(FOLD):
            for k, ref in enumerate((gx, gy)):
                slot = (2 * j + k) * SLOT
                head = jnp.where(lane < 8, lane_roll(both, -slot), 0.0)
                tail = lane_roll(both, LANES - 16 - slot)
                ref[nw, pl.ds(low + j * size, size), :] = jnp.where(
                    lane >= LANES - 8, tail, head
                )
        stages(c, second_round, 0, (8, 16))

    for c in range(chunks):
        when_sent(has_next, to_next[c])
        when_sent(has_prev, to_prev[c])
    when_sent(has_up, up)
    when_sent(has_down, down)
    when_sent(has_right, [col_right])
    when_sent(has_left, [col_left])
    when_sent(has_prev, sum(tile_b, []) + forward_rows + forward_cols)


def pack_rim(field, rim, low, high, first, nw):
    size = (high - low) // FOLD
    lane = lax.broadcasted_iota(jnp.int32, (size, LANES), 1)
    out = jnp.zeros((size, LANES), jnp.float32)
    for j in range(FOLD):
        at = pl.ds(low + j * size, size)
        for k in range(2):
            slot = (2 * j + k) * SLOT
            block = field[k, nw, at, :]
            head, tail = lane_roll(block, slot), lane_roll(block, slot + SLOT)
            out = jnp.where((lane >= slot) & (lane < slot + 8), head, out)
            out = jnp.where((lane >= slot + 8) & (lane < slot + 16), tail, out)
    rim[pl.ds((low - first) // FOLD, size), :] = out


def store(tensor, field, tensor_out, field_out, sem):
    pairs = ((tensor, tensor_out), (field, field_out))
    copies = [
        pltpu.make_async_copy(src.at[k], dst.at[k], sem.at[i, k])
        for i, (src, dst) in enumerate(pairs)
        for k in range(src.shape[0])
    ]
    for copy in copies:
        copy.start()
    for copy in copies:
        copy.wait()


def local(counts, images, stiffness):
    _, rows, width = images.shape
    nw = width // LANES
    nb = nw + 1
    total = rows + 2 * EDGE
    f32 = jnp.float32
    plane = pltpu.VMEM((nb, total, LANES), f32)
    five = pltpu.VMEM((5, nb, total, LANES), f32)
    pair = pltpu.VMEM((2, nb, total, LANES), f32)
    packet = pltpu.VMEM(((rows + 2 * HALO) // FOLD, LANES), f32)
    mains = pltpu.VMEM((2, nw, total, LANES), f32)
    chunks = (rows + 2 * HALO) // CHUNK
    results = pl.pallas_call(
        functools.partial(kernel, counts),
        out_shape=(
            jax.ShapeDtypeStruct((5, 1, rows, width), f32),
            jax.ShapeDtypeStruct((2, 1, rows, width), f32),
        ),
        in_specs=[pl.BlockSpec(memory_space=pltpu.HBM)] * 2,
        out_specs=[pl.BlockSpec(memory_space=pltpu.VMEM)] * 2,
        scratch_shapes=[plane] * 7
        + [five] * 3
        + [plane] * 3
        + [pair] * 7
        + [packet] * 9
        + [mains] * 2
        + [pltpu.VMEM((nb * LANES, nb * LANES), jnp.bfloat16)]
        + [
            pltpu.SemaphoreType.DMA((2, nw)),
            pltpu.SemaphoreType.DMA((KINDS, nw)),
            pltpu.SemaphoreType.DMA((KINDS, nw)),
            pltpu.SemaphoreType.DMA((4, chunks)),
            pltpu.SemaphoreType.DMA((4, chunks)),
            pltpu.SemaphoreType.DMA((chunks, nw)),
            pltpu.SemaphoreType.DMA((chunks, nw)),
        ],
        compiler_params=pltpu.CompilerParams(
            collective_id=0, has_side_effects=True, vmem_limit_bytes=48 * 1024 * 1024
        ),
    )(*(pltpu.with_memory_space_constraint(x, pltpu.HBM) for x in (images, stiffness)))
    return pl.pallas_call(
        store,
        out_shape=tuple(jax.ShapeDtypeStruct(x.shape, f32) for x in results),
        in_specs=[pl.BlockSpec(memory_space=pltpu.VMEM)] * 2,
        out_specs=[pl.BlockSpec(memory_space=pltpu.HBM)] * 2,
        scratch_shapes=[pltpu.SemaphoreType.DMA((2, 5))],
        compiler_params=pltpu.CompilerParams(vmem_limit_bytes=4 * 1024 * 1024),
    )(*results)


def solution(mesh):
    counts = tuple(mesh.shape[name] for name in ("sec", "row", "col"))
    spec = P("sec", "row", "col")
    out = P(None, "sec", "row", "col")
    return jax.shard_map(
        functools.partial(local, counts), mesh=mesh, in_specs=(spec, spec),
        out_specs=(out, out), check_vma=False,
    )
```

```python
import functools

import jax
import jax.numpy as jnp
from jax import lax
from jax.experimental import pallas as pl
from jax.experimental.pallas import tpu as pltpu
from jax.sharding import PartitionSpec as P

RADIUS = 4
SWEEPS = 4
ROUNDS = 2
COUPLING = 0.25
MESH = pl.DeviceIdType.MESH

LANES = 128
HALO = 16
EDGE = HALO + 8
LEAD = 9
GRAD = 16
WIN = 64
SWEEP = 32
EARLY = 2
SLOT = 16
CHUNK = 64
SHORT = 32
FOLD = LANES // (2 * SLOT)

(
    TILE_B, ROW_A_UP, ROW_A_DOWN, ROW_S_UP, ROW_S_DOWN, FWD_TOP, FWD_BOTTOM, COL_RIGHT, COL_LEFT,
    FWD_RIGHT, FWD_LEFT, CORNER, _, _, _, FWD_CORNER, _, _, _,
) = range(19)
KINDS = 19


def bounds_of(rows, first):
    last = first + rows + 2 * HALO
    inside = list(range(first + SHORT, last - SHORT - CHUNK // 2, CHUNK))
    return [first] + inside + [last - SHORT, last]


def lane_roll(x, shift):
    return pltpu.roll(x, shift % x.shape[1], 1)


def columns_of(k):
    return slice(k * LANES, (k + 1) * LANES)


def shifted(blocks, shift, lane):
    rolled = [lane_roll(x, shift) for x in blocks]
    out = []
    for k, here in enumerate(rolled):
        if shift > 0:
            out.append(jnp.where(lane < shift, rolled[k - 1], here))
        else:
            out.append(jnp.where(lane >= LANES + shift, rolled[(k + 1) % len(rolled)], here))
    return out


def add(*terms):
    return [sum(xs[1:], xs[0]) for xs in zip(*terms)]


def kernel(
    counts, images, stiff, tensor_out, field_out,
    a, b, s, q, rq, gx, gy, pr, p3, tt, ca, cb, cc, g0, g1, g2, g3, g4, kk, field,
    send_right, send_left, got_left, got_right, next_left, next_right, corner, next_corner,
    rim, rim_before, rim_after, main_before, main_after, band,
    local_sem, send_sem, recv_sem, chunk_send, chunk_recv, tile_send, tile_recv,
):
    sec, row, col = (lax.axis_index(name) for name in ("sec", "row", "col"))
    n_sec, n_row, n_col = counts
    rows, width = images.shape[1], images.shape[2]
    nb, total, _ = a.shape
    nw = nb - 1
    has_prev, has_next = sec > 0, sec < n_sec - 1
    has_up, has_down = row > 0, row < n_row - 1
    has_left, has_right = col > 0, col < n_col - 1
    sides = (
        (has_prev, (sec - 1, row, col)), (has_next, (sec + 1, row, col)),
        (has_up, (sec, row - 1, col)), (has_down, (sec, row + 1, col)),
        (has_left, (sec, row, col - 1)), (has_right, (sec, row, col + 1)),
    )
    prev_id, next_id, up_id, down_id, left_id, right_id = (side[1] for side in sides)
    corners = tuple(
        (there_row & there_col, (sec, row + step_row, col + step_col))
        for there_row, step_row in ((has_up, -1), (has_down, 1))
        for there_col, step_col in ((has_left, -1), (has_right, 1))
    )
    end = EDGE + rows
    first, last = EDGE - HALO, end + HALO
    inner = pl.ds(EDGE, rows)
    main = pl.ds(0, nw)
    top, bottom = pl.ds(EDGE - HALO, HALO), pl.ds(end, HALO)
    piece = (last - first) // FOLD

    def remote(src, dst, k, device, part=0):
        return pltpu.make_async_remote_copy(
            src_ref=src, dst_ref=dst, send_sem=send_sem.at[k, part],
            recv_sem=recv_sem.at[k, part], device_id=device, device_id_type=MESH,
        )

    def columns(k):
        return pl.ds(k * LANES, LANES)

    loads = [
        pltpu.make_async_copy(src.at[0, :, columns(k)], dst.at[k, inner], local_sem.at[i, k])
        for i, (src, dst) in enumerate(((images, a), (stiff, s)))
        for k in range(nw)
    ]
    for copy in loads:
        copy.start()
    barrier = pltpu.get_barrier_semaphore()
    for there, device in sides + corners:
        @pl.when(there)
        def _():
            pl.semaphore_signal(barrier, inc=1, device_id=device, device_id_type=MESH)

    def clear(ref):
        ref[...] = jnp.zeros(ref.shape, jnp.float32)

    @pl.when(jnp.logical_not(has_up))
    def _():
        clear(a.at[main, top])
        clear(b.at[main, top])
        clear(s.at[main, top])

    @pl.when(jnp.logical_not(has_down))
    def _():
        clear(a.at[main, bottom])
        clear(b.at[main, bottom])
        clear(s.at[main, bottom])

    @pl.when(jnp.logical_not(has_left))
    def _():
        clear(got_left)
        clear(next_left)

    @pl.when(jnp.logical_not(has_right))
    def _():
        clear(got_right)
        clear(next_right)

    for i, (there, _device) in enumerate(corners):
        @pl.when(jnp.logical_not(there))
        def _():
            clear(corner.at[i])
            clear(next_corner.at[i])

    @pl.when(jnp.logical_not(has_next))
    def _():
        clear(b)
        clear(next_corner)
        clear(next_left)
        clear(next_right)
        clear(rim_after)
        clear(main_after)

    @pl.when(jnp.logical_not(has_prev))
    def _():
        clear(rim_before)
        clear(main_before)

    src = lax.broadcasted_iota(jnp.int32, (nb * LANES, nb * LANES), 0)
    dst = lax.broadcasted_iota(jnp.int32, (nb * LANES, nb * LANES), 1)
    fold_at = nw * LANES + LANES // 2
    src = jnp.where(src < fold_at, src, src - nb * LANES)
    dst = jnp.where(dst < fold_at, dst, dst - nb * LANES)
    band[...] = jnp.where(jnp.abs(src - dst) <= RADIUS, 1.0, 0.0).astype(jnp.bfloat16)

    pl.semaphore_wait(barrier, sum(jnp.where(there, 1, 0) for there, _device in sides + corners))

    def by_block(src, at, dst, to, k, device):
        return [
            remote(src.at[0, at, columns(p)], dst.at[p, to], k, device, p) for p in range(nw)
        ]

    low, high = pl.ds(0, HALO), pl.ds(rows - HALO, HALO)
    bounds = bounds_of(rows, first)
    chunks = len(bounds) - 1
    ahead = 8 * (SWEEPS + 1)
    cuts = [0] + [min(high + ahead - EDGE, rows) for high in bounds[1:-1]] + [rows]

    def tile_piece(c):
        if cuts[c] == cuts[c + 1]:
            return []
        at, to = pl.ds(cuts[c], cuts[c + 1] - cuts[c]), pl.ds(EDGE + cuts[c], cuts[c + 1] - cuts[c])
        return [
            pltpu.make_async_remote_copy(
                src_ref=images.at[0, at, columns(p)], dst_ref=b.at[p, to],
                send_sem=tile_send.at[c, p], recv_sem=tile_recv.at[c, p],
                device_id=prev_id, device_id_type=MESH,
            )
            for p in range(nw)
        ]

    tile_b = [tile_piece(c) for c in range(chunks)]
    up = by_block(stiff, low, s, bottom, ROW_S_UP, up_id)
    up += by_block(images, low, a, bottom, ROW_A_UP, up_id)
    down = by_block(stiff, high, s, top, ROW_S_DOWN, down_id)
    down += by_block(images, high, a, top, ROW_A_DOWN, down_id)
    col_right = remote(send_right, got_left, COL_RIGHT, right_id)
    col_left = remote(send_left, got_right, COL_LEFT, left_id)
    forward_rows = [
        (has_up, remote(a.at[main, top], b.at[main, top], FWD_TOP, prev_id)),
        (has_down, remote(a.at[main, bottom], b.at[main, bottom], FWD_BOTTOM, prev_id)),
    ]
    forward_cols = [
        (has_left, remote(got_left, next_left, FWD_LEFT, prev_id)),
        (has_right, remote(got_right, next_right, FWD_RIGHT, prev_id)),
    ] + [
        (there, remote(corner.at[i], next_corner.at[i], FWD_CORNER + i, prev_id))
        for i, (there, _device) in enumerate(corners)
    ]
    head, tail = pl.ds(HALO, HALO), pl.ds(piece - 2 * HALO, HALO)
    to_corner = [
        remote(sent.at[at], corner.at[3 - i], CORNER + i, corners[i][1])
        for i, (sent, at) in enumerate(
            ((send_left, head), (send_right, head), (send_left, tail), (send_right, tail))
        )
    ]

    def when_start(there, copies):
        @pl.when(there)
        def _():
            for copy in copies:
                copy.start()

    def when_got(there, copies):
        @pl.when(there)
        def _():
            for copy in copies:
                copy.wait_recv()

    def when_sent(there, copies):
        @pl.when(there)
        def _():
            for copy in copies:
                copy.wait_send()

    when_start(has_up, up)
    when_start(has_down, down)
    when_start(has_prev, sum(tile_b[:EARLY], []))
    for copy in loads:
        copy.wait()
    def lanes_of(count):
        return lax.broadcasted_iota(jnp.int32, (count, LANES), 1)

    def packed(to, block, at):
        for low, high, folds in (
            (0, HALO, range(1, FOLD)), (HALO, piece - HALO, range(FOLD)),
            (piece - HALO, piece, range(FOLD - 1)),
        ):
            lane = lanes_of(high - low)
            out = jnp.zeros((high - low, LANES), jnp.float32)
            for j in folds:
                span = pl.ds(first + j * piece + low, high - low)
                for k, ref in enumerate((a, s)):
                    slot = (2 * j + k) * SLOT
                    moved = lane_roll(ref[block, span, :], slot - at)
                    out = jnp.where((lane >= slot) & (lane < slot + SLOT), moved, out)
            to[pl.ds(low, high - low), :] = out

    def rim_of(left, right, j, k):
        lane = lanes_of(right.shape[0])
        slot = (2 * j + k) * SLOT
        from_right = jnp.where(lane < SLOT, lane_roll(right, -slot), 0.0)
        return jnp.where(lane >= LANES - SLOT, lane_roll(left, LANES - SLOT - slot), from_right)

    def unpack(ref, left, right, around, k):
        for j in range(FOLD):
            low = HALO if j == 0 else 0
            high = piece - HALO if j == FOLD - 1 else piece
            at = pl.ds(low, high - low)
            ref[nw, pl.ds(first + j * piece + low, high - low), :] = rim_of(
                left[at, :], right[at, :], j, k
            )
        ref[nw, top, :] = rim_of(around[0], around[1], FOLD - 1, k)
        ref[nw, bottom, :] = rim_of(around[2], around[3], 0, k)

    @pl.when(has_right)
    def _():
        packed(send_right, nw - 1, LANES - SLOT)
        col_right.start()

    @pl.when(has_left)
    def _():
        packed(send_left, 0, 0)
        col_left.start()

    for (there, _device), copy in zip(corners, to_corner):
        when_start(there, [copy])
    when_got(has_up, down)
    when_got(has_down, up)
    for there, copy in forward_rows:
        when_start(has_prev & there, [copy])
    when_start(has_prev, sum(tile_b[EARLY:EARLY + 1], []))
    when_got(has_left, [col_right])
    when_got(has_right, [col_left])
    for (there, _device), copy in zip(corners, reversed(to_corner)):
        when_got(there, [copy])
    for there, copy in forward_cols:
        when_start(has_prev & there, [copy])
    when_start(has_prev, sum(tile_b[EARLY + 1:], []))
    unpack(a, got_left, got_right, corner, 0)
    unpack(s, got_left, got_right, corner, 1)

    def get(ref, r, step, *lead):
        return [ref[(*lead, k, pl.ds(r, step), slice(None))] for k in range(nb)]

    def put(ref, values, r, step, *lead):
        for k, value in enumerate(values):
            ref[(*lead, k, pl.ds(r, step), slice(None))] = value

    def blocks(low, high, step, body):
        for r in range(low, high, step):
            body(r, min(step, high - r))

    def gradient(r, step):
        lane = lanes_of(step)
        rim_ok = ((lane < LANES // 2) & has_right) | ((lane >= LANES // 2) & has_left)
        mid = get(a, r, step)
        after, before = shifted(mid, -1, lane), shifted(mid, 1, lane)
        under, over = get(a, r + 1, step), get(a, r - 1, step)
        dx = [x - y for x, y in zip(after, before)]
        dy = [x - y for x, y in zip(under, over)]
        dx[nw], dy[nw] = jnp.where(rim_ok, dx[nw], 0.0), jnp.where(rim_ok, dy[nw], 0.0)
        put(gx, dx, r, step)
        put(gy, dy, r, step)
        put(pr, [x * x for x in dx], r, step, 0)
        put(pr, [x * y for x, y in zip(dx, dy)], r, step, 1)
        put(pr, [y * y for y in dy], r, step, 2)
        stiff_here = get(s, r, step)
        inverse = [lax.rsqrt(jnp.maximum(x, 0.05)) for x in stiff_here]
        put(rq, inverse, r, step)
        put(q, [x * y for x, y in zip(stiff_here, inverse)], r, step)

    def three_rows(ks):
        def body(r, step):
            for k in ks:
                put(p3, add(*(get(pr, r + d, step, k) for d in (-1, 0, 1))), r, step, k)

        return body

    kept = jnp.where(has_next, jnp.float32(1.0), jnp.float32(0.0))
    cells = float((2 * RADIUS + 1) ** 2)

    def window(low, high, ks, factor):
        scale = kept * (factor / cells)

        def body(r, step):
            parts = []
            for k in ks:
                x = jnp.concatenate(add(*(get(p3, r + d, step, k) for d in (-3, 0, 3))), axis=1)
                coarse = x.astype(jnp.bfloat16)
                parts += [coarse, (x - coarse.astype(jnp.float32)).astype(jnp.bfloat16)]
            y = jnp.dot(
                jnp.concatenate(parts, axis=0), band[...], preferred_element_type=jnp.float32
            )
            for i, k in enumerate(ks):
                z = y[2 * i * step:(2 * i + 1) * step] + y[(2 * i + 1) * step:(2 * i + 2) * step]
                value = [z[:, columns_of(j)] * scale for j in range(nb)]
                put(tt, value, r, step, k)
                if EDGE <= r < end:
                    for j in range(nw):
                        tensor_out[k, 0, pl.ds(r - EDGE, step), columns(j)] = value[j]

        if low < EDGE:
            body(low, EDGE - low)
        blocks(max(low, EDGE), min(high, end), WIN, body)
        if high > end:
            body(end, high - end)


    settled = 8 * (SWEEPS - 1)

    def span(c, ahead, margin):
        low = first + margin if c == 0 else bounds[c] + ahead
        high = last - margin if c == chunks - 1 else min(bounds[c + 1] + ahead, last - margin)
        return min(low, high), high

    def beyond_grid(there, at):
        @pl.when(jnp.logical_not(there))
        def _():
            for ref in (gx, gy):
                clear(ref.at[:, at])
            clear(pr.at[pl.ds(0, 3), :, at])

    def own_products(c):
        low, high = span(c, settled + 16, 0)
        blocks(low, high, GRAD, gradient)
        if c == 0:
            beyond_grid(has_up, top)
        if low < last == high:
            beyond_grid(has_down, bottom)
        blocks(*span(c, settled + 8, 0), 16, three_rows((0, 1, 2)))
        window(*span(c, settled, 8), (0, 1, 2), 0.25)

    def change(r, step):
        moved = [x - y for x, y in zip(get(b, r, step), get(a, r, step))]
        put(pr, [x * y for x, y in zip(get(gx, r, step), moved)], r, step, 3)
        put(pr, [x * y for x, y in zip(get(gy, r, step), moved)], r, step, 4)

    def near(source, r, step, part, count):
        mid = get(source, r, step, part)
        lane = lanes_of(step)
        return add(
            get(source, r - 1, step, part), get(source, r + 1, step, part),
            shifted(mid, 1, lane), shifted(mid, -1, lane),
        )[:count]

    def relaxed(source, r, step, start, count):
        nx, ny = (near(source, r, step, part, count) for part in range(2))
        xx, xy, yy = (get(ref, r, step)[:count] for ref in (ca, cb, cc))
        x, y = start
        return (
            [x[k] + (xx[k] * nx[k] - xy[k] * ny[k]) for k in range(count)],
            [y[k] + (yy[k] * ny[k] - xy[k] * nx[k]) for k in range(count)],
        )

    def setup(r, step):
        lane = lanes_of(step)
        xx, xy, yy, xt, yt = (get(tt, r, step, k) for k in range(5))
        mid = get(q, r, step)
        around = add(
            get(q, r - 1, step), get(q, r + 1, step), shifted(mid, 1, lane), shifted(mid, -1, lane)
        )
        at = pl.ds(r, step)
        for k in range(nb):
            diag = mid[k] * around[k] + 2.0 * COUPLING
            one, two = xx[k] + diag, yy[k] + diag
            inverse = mid[k] / (one * two - xy[k] * xy[k])
            xa, xb, xc = two * inverse, xy[k] * inverse, one * inverse
            g0[0, k, at, :] = xb * yt[k] - xa * xt[k]
            g0[1, k, at, :] = xb * xt[k] - xc * yt[k]
            for ref, value in ((ca, xa), (cb, xb), (cc, xc)):
                ref[k, at, :] = value * mid[k]

    def sweep(source, start, target, unscaled=None):
        def body(r, step):
            new = relaxed(
                source, r, step, [get(start, r, step, part) for part in range(2)], nb
            )
            here = get(rq, r, step) if unscaled is not None else None
            for part in range(2):
                if target is not None:
                    put(target, new[part], r, step, part)
                if unscaled is not None:
                    put(unscaled, [x * y for x, y in zip(new[part], here)], r, step, part)

        return body

    def stages(c, bodies, lead, ends):
        for k, body in enumerate(bodies):
            margin = ends[k == len(bodies) - 1]
            low, high = span(c, 8 * (lead - k), margin)
            blocks(max(low, first + margin), high, SWEEP, body)

    first_round = [setup, sweep(g0, g0, g1), sweep(g1, g0, g2), sweep(g2, g0, g3, field)]

    to_next, to_prev = [], []
    for c in range(min(LEAD, chunks)):
        own_products(c)
    for c in range(chunks):
        when_got(has_next, tile_b[c])
        if c == 0:
            for there, copy in forward_rows + forward_cols:
                when_got(has_next & there, [copy])
            unpack(b, next_left, next_right, next_corner, 0)
        blocks(*span(c, settled + 16, 0), 32, change)
        blocks(*span(c, settled + 8, 0), 16, three_rows((3, 4)))
        window(*span(c, settled, 8), (3, 4), 0.5)
        stages(c, first_round, SWEEPS - 1, (8, 8))
        low, high = bounds[c], bounds[c + 1]
        folded = pl.ds((low - first) // FOLD, (high - low) // FOLD)
        pack_rim(field, rim, low, high, first, nw)
        rows_sent = pl.ds(max(low, first + 8), min(high, last - 8) - max(low, first + 8))

        def moves(rims, mains, device, way):
            pairs = (
                (rim.at[folded], rims.at[folded]),
                (field.at[:, main, rows_sent], mains.at[:, main, rows_sent]),
            )
            return [
                pltpu.make_async_remote_copy(
                    src_ref=src, dst_ref=dst, send_sem=chunk_send.at[way + i, c],
                    recv_sem=chunk_recv.at[way + i, c], device_id=device, device_id_type=MESH,
                )
                for i, (src, dst) in enumerate(pairs)
            ]

        to_next.append(moves(rim_before, main_before, next_id, 0))
        to_prev.append(moves(rim_after, main_after, prev_id, 2))
        when_start(has_next, to_next[c])
        when_start(has_prev, to_prev[c])
        if c + LEAD < chunks:
            own_products(c + LEAD)

    def coupled(r, step):
        at = pl.ds(r, step)

        def beside(part, ref):
            return [
                main_before[part, k, at, :] + main_after[part, k, at, :] for k in range(nw)
            ] + [ref[nw, at, :]]

        x, y = beside(0, gx), beside(1, gy)
        xx, xy, yy = (get(ref, r, step) for ref in (ca, cb, cc))
        weight = [v * COUPLING for v in get(rq, r, step)]
        old = [get(g0, r, step, part) for part in range(2)]
        start = (
            [old[0][k] + weight[k] * (xx[k] * x[k] - xy[k] * y[k]) for k in range(nb)],
            [old[1][k] + weight[k] * (yy[k] * y[k] - xy[k] * x[k]) for k in range(nb)],
        )
        new = relaxed(g3, r, step, start, nb)
        for part in range(2):
            put(kk, start[part], r, step, part)
            put(g1, new[part], r, step, part)

    def final(r, step):
        start = [get(kk, r, step, part) for part in range(2)]
        new = relaxed(g4, r, step, start, nw)
        here = get(rq, r, step)
        for part in range(2):
            for k in range(nw):
                field_out[part, 0, pl.ds(r - EDGE, step), columns(k)] = new[part][k] * here[k]

    second_round = [coupled, sweep(g1, kk, g2), sweep(g2, kk, g4), final]
    for c in range(chunks):
        when_got(has_prev, to_next[c])
        when_got(has_next, to_prev[c])
        low, high = bounds[c], bounds[c + 1]
        size = (high - low) // FOLD
        folded = pl.ds((low - first) // FOLD, size)
        both = rim_before[folded, :] + rim_after[folded, :]
        lane = lanes_of(size)
        for j in range(FOLD):
            for k, ref in enumerate((gx, gy)):
                slot = (2 * j + k) * SLOT
                head = jnp.where(lane < 8, lane_roll(both, -slot), 0.0)
                tail = lane_roll(both, LANES - 16 - slot)
                ref[nw, pl.ds(low + j * size, size), :] = jnp.where(
                    lane >= LANES - 8, tail, head
                )
        stages(c, second_round, 0, (8, 16))

    for c in range(chunks):
        when_sent(has_next, to_next[c])
        when_sent(has_prev, to_prev[c])
    when_sent(has_up, up)
    when_sent(has_down, down)
    when_sent(has_right, [col_right])
    when_sent(has_left, [col_left])
    for (there, _device), copy in zip(corners, to_corner):
        when_sent(there, [copy])
    when_sent(has_prev, sum(tile_b, []))
    for there, copy in forward_rows + forward_cols:
        when_sent(has_prev & there, [copy])


def pack_rim(field, rim, low, high, first, nw):
    size = (high - low) // FOLD
    lane = lax.broadcasted_iota(jnp.int32, (size, LANES), 1)
    out = jnp.zeros((size, LANES), jnp.float32)
    for j in range(FOLD):
        at = pl.ds(low + j * size, size)
        for k in range(2):
            slot = (2 * j + k) * SLOT
            block = field[k, nw, at, :]
            head, tail = lane_roll(block, slot), lane_roll(block, slot + SLOT)
            out = jnp.where((lane >= slot) & (lane < slot + 8), head, out)
            out = jnp.where((lane >= slot + 8) & (lane < slot + 16), tail, out)
    rim[pl.ds((low - first) // FOLD, size), :] = out


def store(tensor, field, tensor_out, field_out, sem):
    pairs = ((tensor, tensor_out), (field, field_out))
    copies = [
        pltpu.make_async_copy(src.at[k], dst.at[k], sem.at[i, k])
        for i, (src, dst) in enumerate(pairs)
        for k in range(src.shape[0])
    ]
    for copy in copies:
        copy.start()
    for copy in copies:
        copy.wait()


def local(counts, images, stiffness):
    _, rows, width = images.shape
    nw = width // LANES
    nb = nw + 1
    total = rows + 2 * EDGE
    f32 = jnp.float32
    plane = pltpu.VMEM((nb, total, LANES), f32)
    five = pltpu.VMEM((5, nb, total, LANES), f32)
    pair = pltpu.VMEM((2, nb, total, LANES), f32)
    packet = pltpu.VMEM(((rows + 2 * HALO) // FOLD, LANES), f32)
    mains = pltpu.VMEM((2, nw, total, LANES), f32)
    chunks = len(bounds_of(rows, 0)) - 1
    results = pl.pallas_call(
        functools.partial(kernel, counts),
        out_shape=(
            jax.ShapeDtypeStruct((5, 1, rows, width), f32),
            jax.ShapeDtypeStruct((2, 1, rows, width), f32),
        ),
        in_specs=[pl.BlockSpec(memory_space=pltpu.HBM)] * 2,
        out_specs=[pl.BlockSpec(memory_space=pltpu.VMEM)] * 2,
        scratch_shapes=[plane] * 7
        + [five] * 3
        + [plane] * 3
        + [pair] * 7
        + [packet] * 6
        + [pltpu.VMEM((4, HALO, LANES), f32)] * 2
        + [packet] * 3
        + [mains] * 2
        + [pltpu.VMEM((nb * LANES, nb * LANES), jnp.bfloat16)]
        + [
            pltpu.SemaphoreType.DMA((2, nw)),
            pltpu.SemaphoreType.DMA((KINDS, nw)),
            pltpu.SemaphoreType.DMA((KINDS, nw)),
            pltpu.SemaphoreType.DMA((4, chunks)),
            pltpu.SemaphoreType.DMA((4, chunks)),
            pltpu.SemaphoreType.DMA((chunks, nw)),
            pltpu.SemaphoreType.DMA((chunks, nw)),
        ],
        compiler_params=pltpu.CompilerParams(
            collective_id=0, has_side_effects=True, vmem_limit_bytes=48 * 1024 * 1024
        ),
    )(*(pltpu.with_memory_space_constraint(x, pltpu.HBM) for x in (images, stiffness)))
    return pl.pallas_call(
        store,
        out_shape=tuple(jax.ShapeDtypeStruct(x.shape, f32) for x in results),
        in_specs=[pl.BlockSpec(memory_space=pltpu.VMEM)] * 2,
        out_specs=[pl.BlockSpec(memory_space=pltpu.HBM)] * 2,
        scratch_shapes=[pltpu.SemaphoreType.DMA((2, 5))],
        compiler_params=pltpu.CompilerParams(vmem_limit_bytes=4 * 1024 * 1024),
    )(*results)


def solution(mesh):
    counts = tuple(mesh.shape[name] for name in ("sec", "row", "col"))
    spec = P("sec", "row", "col")
    out = P(None, "sec", "row", "col")
    return jax.shard_map(
        functools.partial(local, counts), mesh=mesh, in_specs=(spec, spec),
        out_specs=(out, out), check_vma=False,
    )
```

```python
import functools

import jax
import jax.numpy as jnp
from jax import lax
from jax.experimental import pallas as pl
from jax.experimental.pallas import tpu as pltpu
from jax.sharding import PartitionSpec as P

RADIUS = 4
SWEEPS = 4
ROUNDS = 2
COUPLING = 0.25
MESH = pl.DeviceIdType.MESH

LANES = 128
HALO = 16
EDGE = HALO + 8
LEAD = 9
GRAD = 16
WIN = 128
SWEEP = 16
EARLY = 2
SLOT = 16
CHUNK = 64
SHORT = 32
FOLD = LANES // (2 * SLOT)

(
    TILE_B, ROW_A_UP, ROW_A_DOWN, ROW_S_UP, ROW_S_DOWN, FWD_TOP, FWD_BOTTOM, COL_RIGHT, COL_LEFT,
    FWD_RIGHT, FWD_LEFT, CORNER, _, _, _, FWD_CORNER, _, _, _,
) = range(19)
KINDS = 19


def bounds_of(rows, first):
    last = first + rows + 2 * HALO
    inside = list(range(first + SHORT, last - SHORT - CHUNK // 2, CHUNK))
    return [first] + inside + [last - SHORT, last]


def lane_roll(x, shift):
    return pltpu.roll(x, shift % x.shape[1], 1)


def columns_of(k):
    return slice(k * LANES, (k + 1) * LANES)


def shifted(blocks, shift, lane):
    rolled = [lane_roll(x, shift) for x in blocks]
    out = []
    for k, here in enumerate(rolled):
        if shift > 0:
            out.append(jnp.where(lane < shift, rolled[k - 1], here))
        else:
            out.append(jnp.where(lane >= LANES + shift, rolled[(k + 1) % len(rolled)], here))
    return out


def add(*terms):
    return [sum(xs[1:], xs[0]) for xs in zip(*terms)]


def kernel(
    counts, images, stiff, tensor_out, field_out,
    a, b, s, q, rq, gx, gy, pr, p3, tt, ca, cb, cc, g0, g1, g2, g3, g4, kk, field,
    send_right, send_left, got_left, got_right, next_left, next_right, corner, next_corner,
    rim, rim_before, rim_after, main_before, main_after, band,
    local_sem, send_sem, recv_sem, chunk_send, chunk_recv, tile_send, tile_recv,
):
    sec, row, col = (lax.axis_index(name) for name in ("sec", "row", "col"))
    n_sec, n_row, n_col = counts
    rows, width = images.shape[1], images.shape[2]
    nb, total, _ = a.shape
    nw = nb - 1
    has_prev, has_next = sec > 0, sec < n_sec - 1
    has_up, has_down = row > 0, row < n_row - 1
    has_left, has_right = col > 0, col < n_col - 1
    sides = (
        (has_prev, (sec - 1, row, col)), (has_next, (sec + 1, row, col)),
        (has_up, (sec, row - 1, col)), (has_down, (sec, row + 1, col)),
        (has_left, (sec, row, col - 1)), (has_right, (sec, row, col + 1)),
    )
    prev_id, next_id, up_id, down_id, left_id, right_id = (side[1] for side in sides)
    corners = tuple(
        (there_row & there_col, (sec, row + step_row, col + step_col))
        for there_row, step_row in ((has_up, -1), (has_down, 1))
        for there_col, step_col in ((has_left, -1), (has_right, 1))
    )
    end = EDGE + rows
    first, last = EDGE - HALO, end + HALO
    inner = pl.ds(EDGE, rows)
    main = pl.ds(0, nw)
    top, bottom = pl.ds(EDGE - HALO, HALO), pl.ds(end, HALO)
    piece = (last - first) // FOLD

    def remote(src, dst, k, device, part=0):
        return pltpu.make_async_remote_copy(
            src_ref=src, dst_ref=dst, send_sem=send_sem.at[k, part],
            recv_sem=recv_sem.at[k, part], device_id=device, device_id_type=MESH,
        )

    def columns(k):
        return pl.ds(k * LANES, LANES)

    loads = [
        pltpu.make_async_copy(src.at[0, :, columns(k)], dst.at[k, inner], local_sem.at[i, k])
        for i, (src, dst) in enumerate(((images, a), (stiff, s)))
        for k in range(nw)
    ]
    for copy in loads:
        copy.start()
    barrier = pltpu.get_barrier_semaphore()
    for there, device in sides + corners:
        @pl.when(there)
        def _():
            pl.semaphore_signal(barrier, inc=1, device_id=device, device_id_type=MESH)

    def clear(ref):
        ref[...] = jnp.zeros(ref.shape, jnp.float32)

    @pl.when(jnp.logical_not(has_up))
    def _():
        clear(a.at[main, top])
        clear(b.at[main, top])
        clear(s.at[main, top])

    @pl.when(jnp.logical_not(has_down))
    def _():
        clear(a.at[main, bottom])
        clear(b.at[main, bottom])
        clear(s.at[main, bottom])

    @pl.when(jnp.logical_not(has_left))
    def _():
        clear(got_left)
        clear(next_left)

    @pl.when(jnp.logical_not(has_right))
    def _():
        clear(got_right)
        clear(next_right)

    for i, (there, _device) in enumerate(corners):
        @pl.when(jnp.logical_not(there))
        def _():
            clear(corner.at[i])
            clear(next_corner.at[i])

    @pl.when(jnp.logical_not(has_next))
    def _():
        clear(b)
        clear(next_corner)
        clear(next_left)
        clear(next_right)
        clear(rim_after)
        clear(main_after)

    @pl.when(jnp.logical_not(has_prev))
    def _():
        clear(rim_before)
        clear(main_before)

    src = lax.broadcasted_iota(jnp.int32, (nb * LANES, nb * LANES), 0)
    dst = lax.broadcasted_iota(jnp.int32, (nb * LANES, nb * LANES), 1)
    fold_at = nw * LANES + LANES // 2
    src = jnp.where(src < fold_at, src, src - nb * LANES)
    dst = jnp.where(dst < fold_at, dst, dst - nb * LANES)
    band[...] = jnp.where(jnp.abs(src - dst) <= RADIUS, 1.0, 0.0).astype(jnp.bfloat16)

    def lanes_of(count):
        return lax.broadcasted_iota(jnp.int32, (count, LANES), 1)

    def packed(to, block, at):
        for low, high, folds in (
            (0, HALO, range(1, FOLD)), (HALO, piece - HALO, range(FOLD)),
            (piece - HALO, piece, range(FOLD - 1)),
        ):
            lane = lanes_of(high - low)
            out = jnp.zeros((high - low, LANES), jnp.float32)
            for j in folds:
                span = pl.ds(first + j * piece + low, high - low)
                for k, ref in enumerate((a, s)):
                    slot = (2 * j + k) * SLOT
                    moved = lane_roll(ref[block, span, :], slot - at)
                    out = jnp.where((lane >= slot) & (lane < slot + SLOT), moved, out)
            to[pl.ds(low, high - low), :] = out

    for copy in loads:
        copy.wait()

    @pl.when(has_right)
    def _():
        packed(send_right, nw - 1, LANES - SLOT)

    @pl.when(has_left)
    def _():
        packed(send_left, 0, 0)

    pl.semaphore_wait(barrier, sum(jnp.where(there, 1, 0) for there, _device in sides + corners))

    def by_block(src, at, dst, to, k, device):
        return [
            remote(src.at[0, at, columns(p)], dst.at[p, to], k, device, p) for p in range(nw)
        ]

    low, high = pl.ds(0, HALO), pl.ds(rows - HALO, HALO)
    bounds = bounds_of(rows, first)
    chunks = len(bounds) - 1
    ahead = 8 * (SWEEPS + 1)
    cuts = [0] + [min(high + ahead - EDGE, rows) for high in bounds[1:-1]] + [rows]

    def tile_piece(c):
        if cuts[c] == cuts[c + 1]:
            return []
        at, to = pl.ds(cuts[c], cuts[c + 1] - cuts[c]), pl.ds(EDGE + cuts[c], cuts[c + 1] - cuts[c])
        return [
            pltpu.make_async_remote_copy(
                src_ref=images.at[0, at, columns(p)], dst_ref=b.at[p, to],
                send_sem=tile_send.at[c, p], recv_sem=tile_recv.at[c, p],
                device_id=prev_id, device_id_type=MESH,
            )
            for p in range(nw)
        ]

    tile_b = [tile_piece(c) for c in range(chunks)]
    near = HALO // 2
    up = by_block(stiff, pl.ds(0, near), s, pl.ds(end, near), ROW_S_UP, up_id)
    up += by_block(images, low, a, bottom, ROW_A_UP, up_id)
    down = by_block(
        stiff, pl.ds(rows - near, near), s, pl.ds(EDGE - near, near), ROW_S_DOWN, down_id
    )
    down += by_block(images, high, a, top, ROW_A_DOWN, down_id)
    col_right = remote(send_right, got_left, COL_RIGHT, right_id)
    col_left = remote(send_left, got_right, COL_LEFT, left_id)
    forward_rows = [
        (has_up, remote(a.at[main, top], b.at[main, top], FWD_TOP, prev_id)),
        (has_down, remote(a.at[main, bottom], b.at[main, bottom], FWD_BOTTOM, prev_id)),
    ]
    forward_cols = [
        (has_left, remote(got_left, next_left, FWD_LEFT, prev_id)),
        (has_right, remote(got_right, next_right, FWD_RIGHT, prev_id)),
    ] + [
        (there, remote(corner.at[i], next_corner.at[i], FWD_CORNER + i, prev_id))
        for i, (there, _device) in enumerate(corners)
    ]
    head, tail = pl.ds(HALO, HALO), pl.ds(piece - 2 * HALO, HALO)
    to_corner = [
        remote(sent.at[at], corner.at[3 - i], CORNER + i, corners[i][1])
        for i, (sent, at) in enumerate(
            ((send_left, head), (send_right, head), (send_left, tail), (send_right, tail))
        )
    ]

    def when_start(there, copies):
        @pl.when(there)
        def _():
            for copy in copies:
                copy.start()

    def when_got(there, copies):
        @pl.when(there)
        def _():
            for copy in copies:
                copy.wait_recv()

    def when_sent(there, copies):
        @pl.when(there)
        def _():
            for copy in copies:
                copy.wait_send()

    when_start(has_up, up)
    when_start(has_down, down)
    when_start(has_prev, sum(tile_b[:EARLY], []))
    def rim_of(left, right, j, k):
        lane = lanes_of(right.shape[0])
        slot = (2 * j + k) * SLOT
        from_right = jnp.where(lane < SLOT, lane_roll(right, -slot), 0.0)
        return jnp.where(lane >= LANES - SLOT, lane_roll(left, LANES - SLOT - slot), from_right)

    def unpack(ref, left, right, around, k):
        for j in range(FOLD):
            low = HALO if j == 0 else 0
            high = piece - HALO if j == FOLD - 1 else piece
            at = pl.ds(low, high - low)
            ref[nw, pl.ds(first + j * piece + low, high - low), :] = rim_of(
                left[at, :], right[at, :], j, k
            )
        ref[nw, top, :] = rim_of(around[0], around[1], FOLD - 1, k)
        ref[nw, bottom, :] = rim_of(around[2], around[3], 0, k)

    @pl.when(has_right)
    def _():
        col_right.start()

    @pl.when(has_left)
    def _():
        col_left.start()

    for (there, _device), copy in zip(corners, to_corner):
        when_start(there, [copy])
    when_got(has_up, down)
    when_got(has_down, up)
    for there, copy in forward_rows:
        when_start(has_prev & there, [copy])
    when_start(has_prev, sum(tile_b[EARLY:EARLY + 1], []))
    when_got(has_left, [col_right])
    when_got(has_right, [col_left])
    for (there, _device), copy in zip(corners, reversed(to_corner)):
        when_got(there, [copy])
    for there, copy in forward_cols:
        when_start(has_prev & there, [copy])
    when_start(has_prev, sum(tile_b[EARLY + 1:], []))
    unpack(a, got_left, got_right, corner, 0)
    unpack(s, got_left, got_right, corner, 1)

    def get(ref, r, step, *lead):
        return [ref[(*lead, k, pl.ds(r, step), slice(None))] for k in range(nb)]

    def put(ref, values, r, step, *lead):
        for k, value in enumerate(values):
            ref[(*lead, k, pl.ds(r, step), slice(None))] = value

    def blocks(low, high, step, body):
        for r in range(low, high, step):
            body(r, min(step, high - r))

    def gradient(r, step):
        lane = lanes_of(step)
        rim_ok = ((lane < LANES // 2) & has_right) | ((lane >= LANES // 2) & has_left)
        mid = get(a, r, step)
        after, before = shifted(mid, -1, lane), shifted(mid, 1, lane)
        under, over = get(a, r + 1, step), get(a, r - 1, step)
        dx = [x - y for x, y in zip(after, before)]
        dy = [x - y for x, y in zip(under, over)]
        dx[nw], dy[nw] = jnp.where(rim_ok, dx[nw], 0.0), jnp.where(rim_ok, dy[nw], 0.0)
        put(gx, dx, r, step)
        put(gy, dy, r, step)
        put(pr, [x * x for x in dx], r, step, 0)
        put(pr, [x * y for x, y in zip(dx, dy)], r, step, 1)
        put(pr, [y * y for y in dy], r, step, 2)
        stiff_here = get(s, r, step)
        inverse = [lax.rsqrt(jnp.maximum(x, 0.05)) for x in stiff_here]
        put(rq, inverse, r, step)
        put(q, [x * y for x, y in zip(stiff_here, inverse)], r, step)

    def three_rows(ks):
        def body(r, step):
            for k in ks:
                put(p3, add(*(get(pr, r + d, step, k) for d in (-1, 0, 1))), r, step, k)

        return body

    kept = jnp.where(has_next, jnp.float32(1.0), jnp.float32(0.0))
    cells = float((2 * RADIUS + 1) ** 2)

    def window(low, high, ks, factor):
        scale = kept * (factor / cells)

        def body(r, step):
            parts = []
            for k in ks:
                x = jnp.concatenate(add(*(get(p3, r + d, step, k) for d in (-3, 0, 3))), axis=1)
                coarse = x.astype(jnp.bfloat16)
                parts += [coarse, (x - coarse.astype(jnp.float32)).astype(jnp.bfloat16)]
            y = jnp.dot(
                jnp.concatenate(parts, axis=0), band[...], preferred_element_type=jnp.float32
            )
            for i, k in enumerate(ks):
                z = y[2 * i * step:(2 * i + 1) * step] + y[(2 * i + 1) * step:(2 * i + 2) * step]
                value = [z[:, columns_of(j)] * scale for j in range(nb)]
                put(tt, value, r, step, k)
                if EDGE <= r < end:
                    for j in range(nw):
                        tensor_out[k, 0, pl.ds(r - EDGE, step), columns(j)] = value[j]

        if low < EDGE:
            body(low, EDGE - low)
        blocks(max(low, EDGE), min(high, end), WIN, body)
        if high > end:
            body(end, high - end)


    settled = 8 * (SWEEPS - 1)

    def span(c, ahead, margin):
        low = first + margin if c == 0 else bounds[c] + ahead
        high = last - margin if c == chunks - 1 else min(bounds[c + 1] + ahead, last - margin)
        return min(low, high), high

    def beyond_grid(there, at):
        @pl.when(jnp.logical_not(there))
        def _():
            for ref in (gx, gy):
                clear(ref.at[:, at])
            clear(pr.at[pl.ds(0, 3), :, at])

    def own_products(c):
        low, high = span(c, settled + 16, 0)
        blocks(low, high, GRAD, gradient)
        if c == 0:
            beyond_grid(has_up, top)
        if low < last == high:
            beyond_grid(has_down, bottom)
        blocks(*span(c, settled + 8, 0), 16, three_rows((0, 1, 2)))
        window(*span(c, settled, 8), (0, 1, 2), 0.25)

    def change(r, step):
        moved = [x - y for x, y in zip(get(b, r, step), get(a, r, step))]
        put(pr, [x * y for x, y in zip(get(gx, r, step), moved)], r, step, 3)
        put(pr, [x * y for x, y in zip(get(gy, r, step), moved)], r, step, 4)

    def near(source, r, step, part, count):
        mid = get(source, r, step, part)
        lane = lanes_of(step)
        return add(
            get(source, r - 1, step, part), get(source, r + 1, step, part),
            shifted(mid, 1, lane), shifted(mid, -1, lane),
        )[:count]

    def relaxed(source, r, step, start, count):
        nx, ny = (near(source, r, step, part, count) for part in range(2))
        xx, xy, yy = (get(ref, r, step)[:count] for ref in (ca, cb, cc))
        x, y = start
        return (
            [x[k] + (xx[k] * nx[k] - xy[k] * ny[k]) for k in range(count)],
            [y[k] + (yy[k] * ny[k] - xy[k] * nx[k]) for k in range(count)],
        )

    def setup(r, step):
        lane = lanes_of(step)
        xx, xy, yy, xt, yt = (get(tt, r, step, k) for k in range(5))
        mid = get(q, r, step)
        around = add(
            get(q, r - 1, step), get(q, r + 1, step), shifted(mid, 1, lane), shifted(mid, -1, lane)
        )
        at = pl.ds(r, step)
        for k in range(nb):
            diag = mid[k] * around[k] + 2.0 * COUPLING
            one, two = xx[k] + diag, yy[k] + diag
            inverse = mid[k] / (one * two - xy[k] * xy[k])
            xa, xb, xc = two * inverse, xy[k] * inverse, one * inverse
            g0[0, k, at, :] = xb * yt[k] - xa * xt[k]
            g0[1, k, at, :] = xb * xt[k] - xc * yt[k]
            for ref, value in ((ca, xa), (cb, xb), (cc, xc)):
                ref[k, at, :] = value * mid[k]

    def sweep(source, start, target, unscaled=None):
        def body(r, step):
            new = relaxed(
                source, r, step, [get(start, r, step, part) for part in range(2)], nb
            )
            here = get(rq, r, step) if unscaled is not None else None
            for part in range(2):
                if target is not None:
                    put(target, new[part], r, step, part)
                if unscaled is not None:
                    put(unscaled, [x * y for x, y in zip(new[part], here)], r, step, part)

        return body

    def stages(c, bodies, lead, ends):
        for k, body in enumerate(bodies):
            margin = ends[k == len(bodies) - 1]
            low, high = span(c, 8 * (lead - k), margin)
            blocks(max(low, first + margin), high, SWEEP, body)

    first_round = [setup, sweep(g0, g0, g1), sweep(g1, g0, g2), sweep(g2, g0, g3, field)]

    to_next, to_prev = [], []
    for c in range(min(LEAD, chunks)):
        own_products(c)
    for c in range(chunks):
        when_got(has_next, tile_b[c])
        if c == 0:
            for there, copy in forward_rows + forward_cols:
                when_got(has_next & there, [copy])
            unpack(b, next_left, next_right, next_corner, 0)
        blocks(*span(c, settled + 16, 0), 32, change)
        blocks(*span(c, settled + 8, 0), 16, three_rows((3, 4)))
        window(*span(c, settled, 8), (3, 4), 0.5)
        stages(c, first_round, SWEEPS - 1, (8, 8))
        low, high = bounds[c], bounds[c + 1]
        folded = pl.ds((low - first) // FOLD, (high - low) // FOLD)
        pack_rim(field, rim, low, high, first, nw)
        rows_sent = pl.ds(max(low, first + 8), min(high, last - 8) - max(low, first + 8))

        def moves(rims, mains, device, way):
            pairs = (
                (rim.at[folded], rims.at[folded]),
                (field.at[:, main, rows_sent], mains.at[:, main, rows_sent]),
            )
            return [
                pltpu.make_async_remote_copy(
                    src_ref=src, dst_ref=dst, send_sem=chunk_send.at[way + i, c],
                    recv_sem=chunk_recv.at[way + i, c], device_id=device, device_id_type=MESH,
                )
                for i, (src, dst) in enumerate(pairs)
            ]

        to_next.append(moves(rim_before, main_before, next_id, 0))
        to_prev.append(moves(rim_after, main_after, prev_id, 2))
        when_start(has_next, to_next[c])
        when_start(has_prev, to_prev[c])
        if c + LEAD < chunks:
            own_products(c + LEAD)

    def coupled(r, step):
        at = pl.ds(r, step)

        def beside(part, ref):
            return [
                main_before[part, k, at, :] + main_after[part, k, at, :] for k in range(nw)
            ] + [ref[nw, at, :]]

        x, y = beside(0, gx), beside(1, gy)
        xx, xy, yy = (get(ref, r, step) for ref in (ca, cb, cc))
        weight = [v * COUPLING for v in get(rq, r, step)]
        old = [get(g0, r, step, part) for part in range(2)]
        start = (
            [old[0][k] + weight[k] * (xx[k] * x[k] - xy[k] * y[k]) for k in range(nb)],
            [old[1][k] + weight[k] * (yy[k] * y[k] - xy[k] * x[k]) for k in range(nb)],
        )
        new = relaxed(g3, r, step, start, nb)
        for part in range(2):
            put(kk, start[part], r, step, part)
            put(g1, new[part], r, step, part)

    def final(r, step):
        start = [get(kk, r, step, part) for part in range(2)]
        new = relaxed(g4, r, step, start, nw)
        here = get(rq, r, step)
        for part in range(2):
            for k in range(nw):
                field_out[part, 0, pl.ds(r - EDGE, step), columns(k)] = new[part][k] * here[k]

    second_round = [coupled, sweep(g1, kk, g2), sweep(g2, kk, g4), final]
    for c in range(chunks):
        when_got(has_prev, to_next[c])
        when_got(has_next, to_prev[c])
        low, high = bounds[c], bounds[c + 1]
        size = (high - low) // FOLD
        folded = pl.ds((low - first) // FOLD, size)
        both = rim_before[folded, :] + rim_after[folded, :]
        lane = lanes_of(size)
        for j in range(FOLD):
            for k, ref in enumerate((gx, gy)):
                slot = (2 * j + k) * SLOT
                head = jnp.where(lane < 8, lane_roll(both, -slot), 0.0)
                tail = lane_roll(both, LANES - 16 - slot)
                ref[nw, pl.ds(low + j * size, size), :] = jnp.where(
                    lane >= LANES - 8, tail, head
                )
        stages(c, second_round, 0, (8, 16))

    for c in range(chunks):
        when_sent(has_next, to_next[c])
        when_sent(has_prev, to_prev[c])
    when_sent(has_up, up)
    when_sent(has_down, down)
    when_sent(has_right, [col_right])
    when_sent(has_left, [col_left])
    for (there, _device), copy in zip(corners, to_corner):
        when_sent(there, [copy])
    when_sent(has_prev, sum(tile_b, []))
    for there, copy in forward_rows + forward_cols:
        when_sent(has_prev & there, [copy])


def pack_rim(field, rim, low, high, first, nw):
    size = (high - low) // FOLD
    lane = lax.broadcasted_iota(jnp.int32, (size, LANES), 1)
    out = jnp.zeros((size, LANES), jnp.float32)
    for j in range(FOLD):
        at = pl.ds(low + j * size, size)
        for k in range(2):
            slot = (2 * j + k) * SLOT
            block = field[k, nw, at, :]
            head, tail = lane_roll(block, slot), lane_roll(block, slot + SLOT)
            out = jnp.where((lane >= slot) & (lane < slot + 8), head, out)
            out = jnp.where((lane >= slot + 8) & (lane < slot + 16), tail, out)
    rim[pl.ds((low - first) // FOLD, size), :] = out


def store(tensor, field, tensor_out, field_out, sem):
    pairs = ((tensor, tensor_out), (field, field_out))
    copies = [pltpu.make_async_copy(src, dst, sem.at[i]) for i, (src, dst) in enumerate(pairs)]
    for copy in copies:
        copy.start()
    for copy in copies:
        copy.wait()


def local(counts, images, stiffness):
    _, rows, width = images.shape
    nw = width // LANES
    nb = nw + 1
    total = rows + 2 * EDGE
    f32 = jnp.float32
    plane = pltpu.VMEM((nb, total, LANES), f32)
    five = pltpu.VMEM((5, nb, total, LANES), f32)
    pair = pltpu.VMEM((2, nb, total, LANES), f32)
    packet = pltpu.VMEM(((rows + 2 * HALO) // FOLD, LANES), f32)
    mains = pltpu.VMEM((2, nw, total, LANES), f32)
    chunks = len(bounds_of(rows, 0)) - 1
    results = pl.pallas_call(
        functools.partial(kernel, counts),
        out_shape=(
            jax.ShapeDtypeStruct((5, 1, rows, width), f32),
            jax.ShapeDtypeStruct((2, 1, rows, width), f32),
        ),
        in_specs=[pl.BlockSpec(memory_space=pltpu.HBM)] * 2,
        out_specs=[pl.BlockSpec(memory_space=pltpu.VMEM)] * 2,
        scratch_shapes=[plane] * 7
        + [five] * 3
        + [plane] * 3
        + [pair] * 7
        + [packet] * 6
        + [pltpu.VMEM((4, HALO, LANES), f32)] * 2
        + [packet] * 3
        + [mains] * 2
        + [pltpu.VMEM((nb * LANES, nb * LANES), jnp.bfloat16)]
        + [
            pltpu.SemaphoreType.DMA((2, nw)),
            pltpu.SemaphoreType.DMA((KINDS, nw)),
            pltpu.SemaphoreType.DMA((KINDS, nw)),
            pltpu.SemaphoreType.DMA((4, chunks)),
            pltpu.SemaphoreType.DMA((4, chunks)),
            pltpu.SemaphoreType.DMA((chunks, nw)),
            pltpu.SemaphoreType.DMA((chunks, nw)),
        ],
        compiler_params=pltpu.CompilerParams(
            collective_id=0, has_side_effects=True, vmem_limit_bytes=48 * 1024 * 1024
        ),
    )(*(pltpu.with_memory_space_constraint(x, pltpu.HBM) for x in (images, stiffness)))
    return pl.pallas_call(
        store,
        out_shape=tuple(jax.ShapeDtypeStruct(x.shape, f32) for x in results),
        in_specs=[pl.BlockSpec(memory_space=pltpu.VMEM)] * 2,
        out_specs=[pl.BlockSpec(memory_space=pltpu.HBM)] * 2,
        scratch_shapes=[pltpu.SemaphoreType.DMA((2,))],
        compiler_params=pltpu.CompilerParams(vmem_limit_bytes=4 * 1024 * 1024),
    )(*results)


def solution(mesh):
    counts = tuple(mesh.shape[name] for name in ("sec", "row", "col"))
    spec = P("sec", "row", "col")
    out = P(None, "sec", "row", "col")
    return jax.shard_map(
        functools.partial(local, counts), mesh=mesh, in_specs=(spec, spec),
        out_specs=(out, out), check_vma=False,
    )
```

```python
import functools

import jax
import jax.numpy as jnp
from jax import lax
from jax.experimental import pallas as pl
from jax.experimental.pallas import tpu as pltpu
from jax.sharding import PartitionSpec as P

RADIUS = 4
SWEEPS = 4
ROUNDS = 2
COUPLING = 0.25
MESH = pl.DeviceIdType.MESH

LANES = 128
HALO = 16
EDGE = HALO + 8
LEAD = 9
GRAD = 16
WIN = 128
SWEEP = 16
EARLY = 1
SLOT = 16
CHUNK = 64
SHORT = 64
FOLD = LANES // (2 * SLOT)

(
    TILE_B, ROW_A_UP, ROW_A_DOWN, ROW_S_UP, ROW_S_DOWN, FWD_TOP, FWD_BOTTOM, COL_RIGHT, COL_LEFT,
    FWD_RIGHT, FWD_LEFT, CORNER, _, _, _, FWD_CORNER, _, _, _,
) = range(19)
KINDS = 19


def bounds_of(rows, first):
    last = first + rows + 2 * HALO
    inside = list(range(first + SHORT, last - SHORT - CHUNK // 2, CHUNK))
    return [first] + inside + [last - SHORT, last]


def lane_roll(x, shift):
    return pltpu.roll(x, shift % x.shape[1], 1)


def columns_of(k):
    return slice(k * LANES, (k + 1) * LANES)


def shifted(blocks, shift, lane):
    rolled = [lane_roll(x, shift) for x in blocks]
    out = []
    for k, here in enumerate(rolled):
        if shift > 0:
            out.append(jnp.where(lane < shift, rolled[k - 1], here))
        else:
            out.append(jnp.where(lane >= LANES + shift, rolled[(k + 1) % len(rolled)], here))
    return out


def add(*terms):
    return [sum(xs[1:], xs[0]) for xs in zip(*terms)]


def kernel(
    counts, images, stiff, tensor_out, field_out,
    a, b, s, q, rq, gx, gy, pr, p3, tt, ca, cb, cc, g0, g1, g2, g3, g4, kk, field,
    send_right, send_left, got_left, got_right, next_left, next_right, corner, next_corner,
    rim, rim_before, rim_after, main_before, main_after, band,
    local_sem, send_sem, recv_sem, chunk_send, chunk_recv, tile_send, tile_recv,
):
    sec, row, col = (lax.axis_index(name) for name in ("sec", "row", "col"))
    n_sec, n_row, n_col = counts
    rows, width = images.shape[1], images.shape[2]
    nb, total, _ = a.shape
    nw = nb - 1
    has_prev, has_next = sec > 0, sec < n_sec - 1
    has_up, has_down = row > 0, row < n_row - 1
    has_left, has_right = col > 0, col < n_col - 1
    sides = (
        (has_prev, (sec - 1, row, col)), (has_next, (sec + 1, row, col)),
        (has_up, (sec, row - 1, col)), (has_down, (sec, row + 1, col)),
        (has_left, (sec, row, col - 1)), (has_right, (sec, row, col + 1)),
    )
    prev_id, next_id, up_id, down_id, left_id, right_id = (side[1] for side in sides)
    corners = tuple(
        (there_row & there_col, (sec, row + step_row, col + step_col))
        for there_row, step_row in ((has_up, -1), (has_down, 1))
        for there_col, step_col in ((has_left, -1), (has_right, 1))
    )
    end = EDGE + rows
    first, last = EDGE - HALO, end + HALO
    inner = pl.ds(EDGE, rows)
    main = pl.ds(0, nw)
    top, bottom = pl.ds(EDGE - HALO, HALO), pl.ds(end, HALO)
    piece = (last - first) // FOLD

    def remote(src, dst, k, device, part=0):
        return pltpu.make_async_remote_copy(
            src_ref=src, dst_ref=dst, send_sem=send_sem.at[k, part],
            recv_sem=recv_sem.at[k, part], device_id=device, device_id_type=MESH,
        )

    def columns(k):
        return pl.ds(k * LANES, LANES)

    loads = [
        pltpu.make_async_copy(src.at[0, :, columns(k)], dst.at[k, inner], local_sem.at[i, k])
        for i, (src, dst) in enumerate(((images, a), (stiff, s)))
        for k in range(nw)
    ]
    for copy in loads:
        copy.start()
    barrier = pltpu.get_barrier_semaphore()
    for there, device in sides + corners:
        @pl.when(there)
        def _():
            pl.semaphore_signal(barrier, inc=1, device_id=device, device_id_type=MESH)

    def clear(ref):
        ref[...] = jnp.zeros(ref.shape, jnp.float32)

    @pl.when(jnp.logical_not(has_up))
    def _():
        clear(a.at[main, top])
        clear(b.at[main, top])
        clear(s.at[main, top])

    @pl.when(jnp.logical_not(has_down))
    def _():
        clear(a.at[main, bottom])
        clear(b.at[main, bottom])
        clear(s.at[main, bottom])

    @pl.when(jnp.logical_not(has_left))
    def _():
        clear(got_left)
        clear(next_left)

    @pl.when(jnp.logical_not(has_right))
    def _():
        clear(got_right)
        clear(next_right)

    for i, (there, _device) in enumerate(corners):
        @pl.when(jnp.logical_not(there))
        def _():
            clear(corner.at[i])
            clear(next_corner.at[i])

    @pl.when(jnp.logical_not(has_next))
    def _():
        clear(b)
        clear(next_corner)
        clear(next_left)
        clear(next_right)
        clear(rim_after)
        clear(main_after)

    @pl.when(jnp.logical_not(has_prev))
    def _():
        clear(rim_before)
        clear(main_before)

    src = lax.broadcasted_iota(jnp.int32, (nb * LANES, nb * LANES), 0)
    dst = lax.broadcasted_iota(jnp.int32, (nb * LANES, nb * LANES), 1)
    fold_at = nw * LANES + LANES // 2
    src = jnp.where(src < fold_at, src, src - nb * LANES)
    dst = jnp.where(dst < fold_at, dst, dst - nb * LANES)
    band[...] = jnp.where(jnp.abs(src - dst) <= RADIUS, 1.0, 0.0).astype(jnp.bfloat16)

    def lanes_of(count):
        return lax.broadcasted_iota(jnp.int32, (count, LANES), 1)

    def packed(to, block, at):
        for low, high, folds in (
            (0, HALO, range(1, FOLD)), (HALO, piece - HALO, range(FOLD)),
            (piece - HALO, piece, range(FOLD - 1)),
        ):
            lane = lanes_of(high - low)
            out = jnp.zeros((high - low, LANES), jnp.float32)
            for j in folds:
                span = pl.ds(first + j * piece + low, high - low)
                for k, ref in enumerate((a, s)):
                    slot = (2 * j + k) * SLOT
                    moved = lane_roll(ref[block, span, :], slot - at)
                    out = jnp.where((lane >= slot) & (lane < slot + SLOT), moved, out)
            to[pl.ds(low, high - low), :] = out

    for copy in loads:
        copy.wait()

    @pl.when(has_right)
    def _():
        packed(send_right, nw - 1, LANES - SLOT)

    @pl.when(has_left)
    def _():
        packed(send_left, 0, 0)

    pl.semaphore_wait(barrier, sum(jnp.where(there, 1, 0) for there, _device in sides + corners))

    def by_block(src, at, dst, to, k, device):
        return [
            remote(src.at[0, at, columns(p)], dst.at[p, to], k, device, p) for p in range(nw)
        ]

    low, high = pl.ds(0, HALO), pl.ds(rows - HALO, HALO)
    bounds = bounds_of(rows, first)
    chunks = len(bounds) - 1
    ahead = 8 * (SWEEPS + 1)
    cuts = [0] + [min(high + ahead - EDGE, rows) for high in bounds[1:-1]] + [rows]

    def tile_piece(c):
        if cuts[c] == cuts[c + 1]:
            return []
        at, to = pl.ds(cuts[c], cuts[c + 1] - cuts[c]), pl.ds(EDGE + cuts[c], cuts[c + 1] - cuts[c])
        return [
            pltpu.make_async_remote_copy(
                src_ref=images.at[0, at, columns(p)], dst_ref=b.at[p, to],
                send_sem=tile_send.at[c, p], recv_sem=tile_recv.at[c, p],
                device_id=prev_id, device_id_type=MESH,
            )
            for p in range(nw)
        ]

    tile_b = [tile_piece(c) for c in range(chunks)]
    near = HALO // 2
    up = by_block(stiff, pl.ds(0, near), s, pl.ds(end, near), ROW_S_UP, up_id)
    up += by_block(images, low, a, bottom, ROW_A_UP, up_id)
    down = by_block(
        stiff, pl.ds(rows - near, near), s, pl.ds(EDGE - near, near), ROW_S_DOWN, down_id
    )
    down += by_block(images, high, a, top, ROW_A_DOWN, down_id)
    col_right = remote(send_right, got_left, COL_RIGHT, right_id)
    col_left = remote(send_left, got_right, COL_LEFT, left_id)
    forward_rows = [
        (has_up, remote(a.at[main, top], b.at[main, top], FWD_TOP, prev_id)),
        (has_down, remote(a.at[main, bottom], b.at[main, bottom], FWD_BOTTOM, prev_id)),
    ]
    forward_cols = [
        (has_left, remote(got_left, next_left, FWD_LEFT, prev_id)),
        (has_right, remote(got_right, next_right, FWD_RIGHT, prev_id)),
    ] + [
        (there, remote(corner.at[i], next_corner.at[i], FWD_CORNER + i, prev_id))
        for i, (there, _device) in enumerate(corners)
    ]
    head, tail = pl.ds(HALO, HALO), pl.ds(piece - 2 * HALO, HALO)
    to_corner = [
        remote(sent.at[at], corner.at[3 - i], CORNER + i, corners[i][1])
        for i, (sent, at) in enumerate(
            ((send_left, head), (send_right, head), (send_left, tail), (send_right, tail))
        )
    ]

    def when_start(there, copies):
        @pl.when(there)
        def _():
            for copy in copies:
                copy.start()

    def when_got(there, copies):
        @pl.when(there)
        def _():
            for copy in copies:
                copy.wait_recv()

    def when_sent(there, copies):
        @pl.when(there)
        def _():
            for copy in copies:
                copy.wait_send()

    when_start(has_up, up)
    when_start(has_down, down)
    when_start(has_prev, sum(tile_b[:EARLY], []))
    def rim_of(left, right, j, k):
        lane = lanes_of(right.shape[0])
        slot = (2 * j + k) * SLOT
        from_right = jnp.where(lane < SLOT, lane_roll(right, -slot), 0.0)
        return jnp.where(lane >= LANES - SLOT, lane_roll(left, LANES - SLOT - slot), from_right)

    def unpack(ref, left, right, around, k):
        for j in range(FOLD):
            low = HALO if j == 0 else 0
            high = piece - HALO if j == FOLD - 1 else piece
            at = pl.ds(low, high - low)
            ref[nw, pl.ds(first + j * piece + low, high - low), :] = rim_of(
                left[at, :], right[at, :], j, k
            )
        ref[nw, top, :] = rim_of(around[0], around[1], FOLD - 1, k)
        ref[nw, bottom, :] = rim_of(around[2], around[3], 0, k)

    @pl.when(has_right)
    def _():
        col_right.start()

    @pl.when(has_left)
    def _():
        col_left.start()

    for (there, _device), copy in zip(corners, to_corner):
        when_start(there, [copy])
    when_got(has_left, [col_right])
    when_got(has_right, [col_left])
    for there, copy in forward_cols[:2]:
        when_start(has_prev & there, [copy])
    when_got(has_up, down)
    when_got(has_down, up)
    for there, copy in forward_rows:
        when_start(has_prev & there, [copy])
    for (there, _device), copy in zip(corners, reversed(to_corner)):
        when_got(there, [copy])
    for there, copy in forward_cols[2:]:
        when_start(has_prev & there, [copy])
    when_start(has_prev, sum(tile_b[EARLY:], []))
    unpack(a, got_left, got_right, corner, 0)
    unpack(s, got_left, got_right, corner, 1)

    def get(ref, r, step, *lead):
        return [ref[(*lead, k, pl.ds(r, step), slice(None))] for k in range(nb)]

    def put(ref, values, r, step, *lead):
        for k, value in enumerate(values):
            ref[(*lead, k, pl.ds(r, step), slice(None))] = value

    def blocks(low, high, step, body):
        for r in range(low, high, step):
            body(r, min(step, high - r))

    def gradient(r, step):
        lane = lanes_of(step)
        rim_ok = ((lane < LANES // 2) & has_right) | ((lane >= LANES // 2) & has_left)
        mid = get(a, r, step)
        after, before = shifted(mid, -1, lane), shifted(mid, 1, lane)
        under, over = get(a, r + 1, step), get(a, r - 1, step)
        dx = [x - y for x, y in zip(after, before)]
        dy = [x - y for x, y in zip(under, over)]
        dx[nw], dy[nw] = jnp.where(rim_ok, dx[nw], 0.0), jnp.where(rim_ok, dy[nw], 0.0)
        put(gx, dx, r, step)
        put(gy, dy, r, step)
        put(pr, [x * x for x in dx], r, step, 0)
        put(pr, [x * y for x, y in zip(dx, dy)], r, step, 1)
        put(pr, [y * y for y in dy], r, step, 2)
        stiff_here = get(s, r, step)
        inverse = [lax.rsqrt(jnp.maximum(x, 0.05)) for x in stiff_here]
        put(rq, inverse, r, step)
        put(q, [x * y for x, y in zip(stiff_here, inverse)], r, step)

    def three_rows(ks):
        def body(r, step):
            for k in ks:
                put(p3, add(*(get(pr, r + d, step, k) for d in (-1, 0, 1))), r, step, k)

        return body

    kept = jnp.where(has_next, jnp.float32(1.0), jnp.float32(0.0))
    cells = float((2 * RADIUS + 1) ** 2)

    def window(low, high, ks, factor):
        scale = kept * (factor / cells)

        def body(r, step):
            parts = []
            for k in ks:
                x = jnp.concatenate(add(*(get(p3, r + d, step, k) for d in (-3, 0, 3))), axis=1)
                coarse = x.astype(jnp.bfloat16)
                parts += [coarse, (x - coarse.astype(jnp.float32)).astype(jnp.bfloat16)]
            y = jnp.dot(
                jnp.concatenate(parts, axis=0), band[...], preferred_element_type=jnp.float32
            )
            for i, k in enumerate(ks):
                z = y[2 * i * step:(2 * i + 1) * step] + y[(2 * i + 1) * step:(2 * i + 2) * step]
                value = [z[:, columns_of(j)] * scale for j in range(nb)]
                put(tt, value, r, step, k)
                if EDGE <= r < end:
                    for j in range(nw):
                        tensor_out[k, 0, pl.ds(r - EDGE, step), columns(j)] = value[j]

        if low < EDGE:
            body(low, EDGE - low)
        blocks(max(low, EDGE), min(high, end), WIN, body)
        if high > end:
            body(end, high - end)


    settled = 8 * (SWEEPS - 1)

    def span(c, ahead, margin):
        low = first + margin if c == 0 else bounds[c] + ahead
        high = last - margin if c == chunks - 1 else min(bounds[c + 1] + ahead, last - margin)
        return min(low, high), high

    def beyond_grid(there, at):
        @pl.when(jnp.logical_not(there))
        def _():
            for ref in (gx, gy):
                clear(ref.at[:, at])
            clear(pr.at[pl.ds(0, 3), :, at])

    def own_products(c):
        low, high = span(c, settled + 16, 0)
        blocks(low, high, GRAD, gradient)
        if c == 0:
            beyond_grid(has_up, top)
        if low < last == high:
            beyond_grid(has_down, bottom)
        blocks(*span(c, settled + 8, 0), 16, three_rows((0, 1, 2)))
        window(*span(c, settled, 8), (0, 1, 2), 0.25)

    def change(r, step):
        moved = [x - y for x, y in zip(get(b, r, step), get(a, r, step))]
        put(pr, [x * y for x, y in zip(get(gx, r, step), moved)], r, step, 3)
        put(pr, [x * y for x, y in zip(get(gy, r, step), moved)], r, step, 4)

    def near(source, r, step, part, count):
        mid = get(source, r, step, part)
        lane = lanes_of(step)
        return add(
            get(source, r - 1, step, part), get(source, r + 1, step, part),
            shifted(mid, 1, lane), shifted(mid, -1, lane),
        )[:count]

    def relaxed(source, r, step, start, count):
        nx, ny = (near(source, r, step, part, count) for part in range(2))
        xx, xy, yy = (get(ref, r, step)[:count] for ref in (ca, cb, cc))
        x, y = start
        return (
            [x[k] + (xx[k] * nx[k] - xy[k] * ny[k]) for k in range(count)],
            [y[k] + (yy[k] * ny[k] - xy[k] * nx[k]) for k in range(count)],
        )

    def setup(r, step):
        lane = lanes_of(step)
        xx, xy, yy, xt, yt = (get(tt, r, step, k) for k in range(5))
        mid = get(q, r, step)
        around = add(
            get(q, r - 1, step), get(q, r + 1, step), shifted(mid, 1, lane), shifted(mid, -1, lane)
        )
        at = pl.ds(r, step)
        for k in range(nb):
            diag = mid[k] * around[k] + 2.0 * COUPLING
            one, two = xx[k] + diag, yy[k] + diag
            inverse = mid[k] / (one * two - xy[k] * xy[k])
            xa, xb, xc = two * inverse, xy[k] * inverse, one * inverse
            g0[0, k, at, :] = xb * yt[k] - xa * xt[k]
            g0[1, k, at, :] = xb * xt[k] - xc * yt[k]
            for ref, value in ((ca, xa), (cb, xb), (cc, xc)):
                ref[k, at, :] = value * mid[k]

    def sweep(source, start, target, unscaled=None):
        def body(r, step):
            new = relaxed(
                source, r, step, [get(start, r, step, part) for part in range(2)], nb
            )
            here = get(rq, r, step) if unscaled is not None else None
            for part in range(2):
                if target is not None:
                    put(target, new[part], r, step, part)
                if unscaled is not None:
                    put(unscaled, [x * y for x, y in zip(new[part], here)], r, step, part)

        return body

    def stages(c, bodies, lead, ends):
        for k, body in enumerate(bodies):
            margin = ends[k == len(bodies) - 1]
            low, high = span(c, 8 * (lead - k), margin)
            blocks(max(low, first + margin), high, SWEEP, body)

    first_round = [setup, sweep(g0, g0, g1), sweep(g1, g0, g2), sweep(g2, g0, g3, field)]

    to_next, to_prev = [], []
    for c in range(min(LEAD, chunks)):
        own_products(c)
    for c in range(chunks):
        when_got(has_next, tile_b[c])
        if c == 0:
            for there, copy in forward_rows + forward_cols:
                when_got(has_next & there, [copy])
            unpack(b, next_left, next_right, next_corner, 0)
        blocks(*span(c, settled + 16, 0), 32, change)
        blocks(*span(c, settled + 8, 0), 16, three_rows((3, 4)))
        window(*span(c, settled, 8), (3, 4), 0.5)
        stages(c, first_round, SWEEPS - 1, (8, 8))
        low, high = bounds[c], bounds[c + 1]
        folded = pl.ds((low - first) // FOLD, (high - low) // FOLD)
        pack_rim(field, rim, low, high, first, nw)
        rows_sent = pl.ds(max(low, first + 8), min(high, last - 8) - max(low, first + 8))

        def moves(rims, mains, device, way):
            pairs = (
                (rim.at[folded], rims.at[folded]),
                (field.at[:, main, rows_sent], mains.at[:, main, rows_sent]),
            )
            return [
                pltpu.make_async_remote_copy(
                    src_ref=src, dst_ref=dst, send_sem=chunk_send.at[way + i, c],
                    recv_sem=chunk_recv.at[way + i, c], device_id=device, device_id_type=MESH,
                )
                for i, (src, dst) in enumerate(pairs)
            ]

        to_next.append(moves(rim_before, main_before, next_id, 0))
        to_prev.append(moves(rim_after, main_after, prev_id, 2))
        when_start(has_next, to_next[c])
        when_start(has_prev, to_prev[c])
        if c + LEAD < chunks:
            own_products(c + LEAD)

    def coupled(r, step):
        at = pl.ds(r, step)

        def beside(part, ref):
            return [
                main_before[part, k, at, :] + main_after[part, k, at, :] for k in range(nw)
            ] + [ref[nw, at, :]]

        x, y = beside(0, gx), beside(1, gy)
        xx, xy, yy = (get(ref, r, step) for ref in (ca, cb, cc))
        weight = [v * COUPLING for v in get(rq, r, step)]
        old = [get(g0, r, step, part) for part in range(2)]
        start = (
            [old[0][k] + weight[k] * (xx[k] * x[k] - xy[k] * y[k]) for k in range(nb)],
            [old[1][k] + weight[k] * (yy[k] * y[k] - xy[k] * x[k]) for k in range(nb)],
        )
        new = relaxed(g3, r, step, start, nb)
        for part in range(2):
            put(kk, start[part], r, step, part)
            put(g1, new[part], r, step, part)

    def final(r, step):
        start = [get(kk, r, step, part) for part in range(2)]
        new = relaxed(g4, r, step, start, nw)
        here = get(rq, r, step)
        for part in range(2):
            for k in range(nw):
                field_out[part, 0, pl.ds(r - EDGE, step), columns(k)] = new[part][k] * here[k]

    second_round = [coupled, sweep(g1, kk, g2), sweep(g2, kk, g4), final]
    for c in range(chunks):
        when_got(has_prev, to_next[c])
        when_got(has_next, to_prev[c])
        low, high = bounds[c], bounds[c + 1]
        size = (high - low) // FOLD
        folded = pl.ds((low - first) // FOLD, size)
        both = rim_before[folded, :] + rim_after[folded, :]
        lane = lanes_of(size)
        for j in range(FOLD):
            for k, ref in enumerate((gx, gy)):
                slot = (2 * j + k) * SLOT
                head = jnp.where(lane < 8, lane_roll(both, -slot), 0.0)
                tail = lane_roll(both, LANES - 16 - slot)
                ref[nw, pl.ds(low + j * size, size), :] = jnp.where(
                    lane >= LANES - 8, tail, head
                )
        stages(c, second_round, 0, (8, 16))

    for c in range(chunks):
        when_sent(has_next, to_next[c])
        when_sent(has_prev, to_prev[c])
    when_sent(has_up, up)
    when_sent(has_down, down)
    when_sent(has_right, [col_right])
    when_sent(has_left, [col_left])
    for (there, _device), copy in zip(corners, to_corner):
        when_sent(there, [copy])
    when_sent(has_prev, sum(tile_b, []))
    for there, copy in forward_rows + forward_cols:
        when_sent(has_prev & there, [copy])


def pack_rim(field, rim, low, high, first, nw):
    size = (high - low) // FOLD
    lane = lax.broadcasted_iota(jnp.int32, (size, LANES), 1)
    out = jnp.zeros((size, LANES), jnp.float32)
    for j in range(FOLD):
        at = pl.ds(low + j * size, size)
        for k in range(2):
            slot = (2 * j + k) * SLOT
            block = field[k, nw, at, :]
            head, tail = lane_roll(block, slot), lane_roll(block, slot + SLOT)
            out = jnp.where((lane >= slot) & (lane < slot + 8), head, out)
            out = jnp.where((lane >= slot + 8) & (lane < slot + 16), tail, out)
    rim[pl.ds((low - first) // FOLD, size), :] = out


def store(tensor, field, tensor_out, field_out, sem):
    pairs = ((tensor, tensor_out), (field, field_out))
    copies = [pltpu.make_async_copy(src, dst, sem.at[i]) for i, (src, dst) in enumerate(pairs)]
    for copy in copies:
        copy.start()
    for copy in copies:
        copy.wait()


def local(counts, images, stiffness):
    _, rows, width = images.shape
    nw = width // LANES
    nb = nw + 1
    total = rows + 2 * EDGE
    f32 = jnp.float32
    plane = pltpu.VMEM((nb, total, LANES), f32)
    five = pltpu.VMEM((5, nb, total, LANES), f32)
    pair = pltpu.VMEM((2, nb, total, LANES), f32)
    packet = pltpu.VMEM(((rows + 2 * HALO) // FOLD, LANES), f32)
    mains = pltpu.VMEM((2, nw, total, LANES), f32)
    chunks = len(bounds_of(rows, 0)) - 1
    results = pl.pallas_call(
        functools.partial(kernel, counts),
        out_shape=(
            jax.ShapeDtypeStruct((5, 1, rows, width), f32),
            jax.ShapeDtypeStruct((2, 1, rows, width), f32),
        ),
        in_specs=[pl.BlockSpec(memory_space=pltpu.HBM)] * 2,
        out_specs=[pl.BlockSpec(memory_space=pltpu.VMEM)] * 2,
        scratch_shapes=[plane] * 7
        + [five] * 3
        + [plane] * 3
        + [pair] * 7
        + [packet] * 6
        + [pltpu.VMEM((4, HALO, LANES), f32)] * 2
        + [packet] * 3
        + [mains] * 2
        + [pltpu.VMEM((nb * LANES, nb * LANES), jnp.bfloat16)]
        + [
            pltpu.SemaphoreType.DMA((2, nw)),
            pltpu.SemaphoreType.DMA((KINDS, nw)),
            pltpu.SemaphoreType.DMA((KINDS, nw)),
            pltpu.SemaphoreType.DMA((4, chunks)),
            pltpu.SemaphoreType.DMA((4, chunks)),
            pltpu.SemaphoreType.DMA((chunks, nw)),
            pltpu.SemaphoreType.DMA((chunks, nw)),
        ],
        compiler_params=pltpu.CompilerParams(
            collective_id=0, has_side_effects=True, vmem_limit_bytes=48 * 1024 * 1024
        ),
    )(*(pltpu.with_memory_space_constraint(x, pltpu.HBM) for x in (images, stiffness)))
    return pl.pallas_call(
        store,
        out_shape=tuple(jax.ShapeDtypeStruct(x.shape, f32) for x in results),
        in_specs=[pl.BlockSpec(memory_space=pltpu.VMEM)] * 2,
        out_specs=[pl.BlockSpec(memory_space=pltpu.HBM)] * 2,
        scratch_shapes=[pltpu.SemaphoreType.DMA((2,))],
        compiler_params=pltpu.CompilerParams(vmem_limit_bytes=4 * 1024 * 1024),
    )(*results)


def solution(mesh):
    counts = tuple(mesh.shape[name] for name in ("sec", "row", "col"))
    spec = P("sec", "row", "col")
    out = P(None, "sec", "row", "col")
    return jax.shard_map(
        functools.partial(local, counts), mesh=mesh, in_specs=(spec, spec),
        out_specs=(out, out), check_vma=False,
    )
```

```python
import functools

import jax
import jax.numpy as jnp
from jax import lax
from jax.experimental import pallas as pl
from jax.experimental.pallas import tpu as pltpu
from jax.sharding import PartitionSpec as P

RADIUS = 4
SWEEPS = 4
ROUNDS = 2
COUPLING = 0.25
MESH = pl.DeviceIdType.MESH

LANES = 128
HALO = 16
EDGE = HALO + 8
LEAD = 9
GRAD = 16
WIN = 128
SWEEP = 16
EARLY = 1
SLOT = 16
CHUNK = 64
SHORT = 64
FOLD = LANES // (2 * SLOT)

(
    TILE_B, ROW_A_UP, ROW_A_DOWN, ROW_S_UP, ROW_S_DOWN, FWD_TOP, FWD_BOTTOM, COL_RIGHT, COL_LEFT,
    FWD_RIGHT, FWD_LEFT, CORNER, _, _, _, FWD_CORNER, _, _, _,
) = range(19)
KINDS = 19


def bounds_of(rows, first):
    last = first + rows + 2 * HALO
    inside = list(range(first + SHORT, last - SHORT - CHUNK // 2, CHUNK))
    return [first] + inside + [last - SHORT, last]


def lane_roll(x, shift):
    return pltpu.roll(x, shift % x.shape[1], 1)


def columns_of(k):
    return slice(k * LANES, (k + 1) * LANES)


def shifted(blocks, shift, lane):
    rolled = [lane_roll(x, shift) for x in blocks]
    out = []
    for k, here in enumerate(rolled):
        if shift > 0:
            out.append(jnp.where(lane < shift, rolled[k - 1], here))
        else:
            out.append(jnp.where(lane >= LANES + shift, rolled[(k + 1) % len(rolled)], here))
    return out


def add(*terms):
    return [sum(xs[1:], xs[0]) for xs in zip(*terms)]


def kernel(
    counts, images, stiff, tensor_out, field_out,
    a, b, s, q, rq, gx, gy, pr, p3, tt, ca, cb, cc, g0, g1, g2, g3, g4, kk, field,
    send_right, send_left, got_left, got_right, next_left, next_right, corner, next_corner,
    rim, rim_before, rim_after, main_before, main_after, band,
    local_sem, send_sem, recv_sem, chunk_send, chunk_recv, tile_send, tile_recv,
):
    sec, row, col = (lax.axis_index(name) for name in ("sec", "row", "col"))
    n_sec, n_row, n_col = counts
    rows, width = images.shape[1], images.shape[2]
    nb, total, _ = a.shape
    nw = nb - 1
    has_prev, has_next = sec > 0, sec < n_sec - 1
    has_up, has_down = row > 0, row < n_row - 1
    has_left, has_right = col > 0, col < n_col - 1
    sides = (
        (has_prev, (sec - 1, row, col)), (has_next, (sec + 1, row, col)),
        (has_up, (sec, row - 1, col)), (has_down, (sec, row + 1, col)),
        (has_left, (sec, row, col - 1)), (has_right, (sec, row, col + 1)),
    )
    prev_id, next_id, up_id, down_id, left_id, right_id = (side[1] for side in sides)
    corners = tuple(
        (there_row & there_col, (sec, row + step_row, col + step_col))
        for there_row, step_row in ((has_up, -1), (has_down, 1))
        for there_col, step_col in ((has_left, -1), (has_right, 1))
    )
    end = EDGE + rows
    first, last = EDGE - HALO, end + HALO
    inner = pl.ds(EDGE, rows)
    main = pl.ds(0, nw)
    top, bottom = pl.ds(EDGE - HALO, HALO), pl.ds(end, HALO)
    piece = (last - first) // FOLD

    def remote(src, dst, k, device, part=0):
        return pltpu.make_async_remote_copy(
            src_ref=src, dst_ref=dst, send_sem=send_sem.at[k, part],
            recv_sem=recv_sem.at[k, part], device_id=device, device_id_type=MESH,
        )

    def columns(k):
        return pl.ds(k * LANES, LANES)

    loads = [
        pltpu.make_async_copy(src.at[0, :, columns(k)], dst.at[k, inner], local_sem.at[i, k])
        for i, (src, dst) in enumerate(((images, a), (stiff, s)))
        for k in range(nw)
    ]
    for copy in loads:
        copy.start()
    barrier = pltpu.get_barrier_semaphore()
    for there, device in sides + corners:
        @pl.when(there)
        def _():
            pl.semaphore_signal(barrier, inc=1, device_id=device, device_id_type=MESH)

    def clear(ref):
        ref[...] = jnp.zeros(ref.shape, jnp.float32)

    @pl.when(jnp.logical_not(has_up))
    def _():
        clear(a.at[main, top])
        clear(b.at[main, top])
        clear(s.at[main, top])

    @pl.when(jnp.logical_not(has_down))
    def _():
        clear(a.at[main, bottom])
        clear(b.at[main, bottom])
        clear(s.at[main, bottom])

    @pl.when(jnp.logical_not(has_left))
    def _():
        clear(got_left)
        clear(next_left)

    @pl.when(jnp.logical_not(has_right))
    def _():
        clear(got_right)
        clear(next_right)

    for i, (there, _device) in enumerate(corners):
        @pl.when(jnp.logical_not(there))
        def _():
            clear(corner.at[i])
            clear(next_corner.at[i])

    @pl.when(jnp.logical_not(has_next))
    def _():
        clear(b)
        clear(next_corner)
        clear(next_left)
        clear(next_right)
        clear(rim_after)
        clear(main_after)

    @pl.when(jnp.logical_not(has_prev))
    def _():
        clear(rim_before)
        clear(main_before)

    src = lax.broadcasted_iota(jnp.int32, (nb * LANES, nb * LANES), 0)
    dst = lax.broadcasted_iota(jnp.int32, (nb * LANES, nb * LANES), 1)
    fold_at = nw * LANES + LANES // 2
    src = jnp.where(src < fold_at, src, src - nb * LANES)
    dst = jnp.where(dst < fold_at, dst, dst - nb * LANES)
    band[...] = jnp.where(jnp.abs(src - dst) <= RADIUS, 1.0, 0.0).astype(jnp.bfloat16)

    def lanes_of(count):
        return lax.broadcasted_iota(jnp.int32, (count, LANES), 1)

    def packed(to, block, at):
        for low, high, folds in (
            (0, HALO, range(1, FOLD)), (HALO, piece - HALO, range(FOLD)),
            (piece - HALO, piece, range(FOLD - 1)),
        ):
            lane = lanes_of(high - low)
            out = jnp.zeros((high - low, LANES), jnp.float32)
            for j in folds:
                span = pl.ds(first + j * piece + low, high - low)
                for k, ref in enumerate((a, s)):
                    slot = (2 * j + k) * SLOT
                    moved = lane_roll(ref[block, span, :], slot - at)
                    out = jnp.where((lane >= slot) & (lane < slot + SLOT), moved, out)
            to[pl.ds(low, high - low), :] = out

    for copy in loads:
        copy.wait()

    @pl.when(has_right)
    def _():
        packed(send_right, nw - 1, LANES - SLOT)

    @pl.when(has_left)
    def _():
        packed(send_left, 0, 0)

    pl.semaphore_wait(barrier, sum(jnp.where(there, 1, 0) for there, _device in sides + corners))

    def by_block(src, at, dst, to, k, device):
        return [
            remote(src.at[0, at, columns(p)], dst.at[p, to], k, device, p) for p in range(nw)
        ]

    low, high = pl.ds(0, HALO), pl.ds(rows - HALO, HALO)
    bounds = bounds_of(rows, first)
    chunks = len(bounds) - 1
    ahead = 8 * (SWEEPS + 1)
    cuts = [0] + [min(high + ahead - EDGE, rows) for high in bounds[1:-1]] + [rows]

    def tile_piece(c):
        if cuts[c] == cuts[c + 1]:
            return []
        at, to = pl.ds(cuts[c], cuts[c + 1] - cuts[c]), pl.ds(EDGE + cuts[c], cuts[c + 1] - cuts[c])
        return [
            pltpu.make_async_remote_copy(
                src_ref=images.at[0, at, columns(p)], dst_ref=b.at[p, to],
                send_sem=tile_send.at[c, p], recv_sem=tile_recv.at[c, p],
                device_id=prev_id, device_id_type=MESH,
            )
            for p in range(nw)
        ]

    tile_b = [tile_piece(c) for c in range(chunks)]
    near = HALO // 2
    up = by_block(stiff, pl.ds(0, near), s, pl.ds(end, near), ROW_S_UP, up_id)
    up += by_block(images, low, a, bottom, ROW_A_UP, up_id)
    down = by_block(
        stiff, pl.ds(rows - near, near), s, pl.ds(EDGE - near, near), ROW_S_DOWN, down_id
    )
    down += by_block(images, high, a, top, ROW_A_DOWN, down_id)
    col_right = remote(send_right, got_left, COL_RIGHT, right_id)
    col_left = remote(send_left, got_right, COL_LEFT, left_id)
    forward_rows = [
        (has_up, remote(a.at[main, top], b.at[main, top], FWD_TOP, prev_id)),
        (has_down, remote(a.at[main, bottom], b.at[main, bottom], FWD_BOTTOM, prev_id)),
    ]
    forward_cols = [
        (has_left, remote(got_left, next_left, FWD_LEFT, prev_id)),
        (has_right, remote(got_right, next_right, FWD_RIGHT, prev_id)),
    ] + [
        (there, remote(corner.at[i], next_corner.at[i], FWD_CORNER + i, prev_id))
        for i, (there, _device) in enumerate(corners)
    ]
    head, tail = pl.ds(HALO, HALO), pl.ds(piece - 2 * HALO, HALO)
    to_corner = [
        remote(sent.at[at], corner.at[3 - i], CORNER + i, corners[i][1])
        for i, (sent, at) in enumerate(
            ((send_left, head), (send_right, head), (send_left, tail), (send_right, tail))
        )
    ]

    def when_start(there, copies):
        @pl.when(there)
        def _():
            for copy in copies:
                copy.start()

    def when_got(there, copies):
        @pl.when(there)
        def _():
            for copy in copies:
                copy.wait_recv()

    def when_sent(there, copies):
        @pl.when(there)
        def _():
            for copy in copies:
                copy.wait_send()

    for (there, _device), copy in zip(corners, to_corner):
        when_start(there, [copy])
    @pl.when(has_right)
    def _():
        col_right.start()

    @pl.when(has_left)
    def _():
        col_left.start()

    when_start(has_up, up)
    when_start(has_down, down)
    when_start(has_prev, sum(tile_b[:EARLY], []))
    def rim_of(left, right, j, k):
        lane = lanes_of(right.shape[0])
        slot = (2 * j + k) * SLOT
        from_right = jnp.where(lane < SLOT, lane_roll(right, -slot), 0.0)
        return jnp.where(lane >= LANES - SLOT, lane_roll(left, LANES - SLOT - slot), from_right)

    def unpack(ref, left, right, around, k):
        for j in range(FOLD):
            low = HALO if j == 0 else 0
            high = piece - HALO if j == FOLD - 1 else piece
            at = pl.ds(low, high - low)
            ref[nw, pl.ds(first + j * piece + low, high - low), :] = rim_of(
                left[at, :], right[at, :], j, k
            )
        ref[nw, top, :] = rim_of(around[0], around[1], FOLD - 1, k)
        ref[nw, bottom, :] = rim_of(around[2], around[3], 0, k)

    when_got(has_left, [col_right])
    when_got(has_right, [col_left])
    for there, copy in forward_cols[:2]:
        when_start(has_prev & there, [copy])
    when_got(has_up, down)
    when_got(has_down, up)
    for there, copy in forward_rows:
        when_start(has_prev & there, [copy])
    for (there, _device), copy in zip(corners, reversed(to_corner)):
        when_got(there, [copy])
    for there, copy in forward_cols[2:]:
        when_start(has_prev & there, [copy])
    when_start(has_prev, sum(tile_b[EARLY:], []))
    unpack(a, got_left, got_right, corner, 0)
    unpack(s, got_left, got_right, corner, 1)

    def get(ref, r, step, *lead):
        return [ref[(*lead, k, pl.ds(r, step), slice(None))] for k in range(nb)]

    def put(ref, values, r, step, *lead):
        for k, value in enumerate(values):
            ref[(*lead, k, pl.ds(r, step), slice(None))] = value

    def blocks(low, high, step, body):
        for r in range(low, high, step):
            body(r, min(step, high - r))

    def gradient(r, step):
        lane = lanes_of(step)
        rim_ok = ((lane < LANES // 2) & has_right) | ((lane >= LANES // 2) & has_left)
        mid = get(a, r, step)
        after, before = shifted(mid, -1, lane), shifted(mid, 1, lane)
        under, over = get(a, r + 1, step), get(a, r - 1, step)
        dx = [x - y for x, y in zip(after, before)]
        dy = [x - y for x, y in zip(under, over)]
        dx[nw], dy[nw] = jnp.where(rim_ok, dx[nw], 0.0), jnp.where(rim_ok, dy[nw], 0.0)
        put(gx, dx, r, step)
        put(gy, dy, r, step)
        put(pr, [x * x for x in dx], r, step, 0)
        put(pr, [x * y for x, y in zip(dx, dy)], r, step, 1)
        put(pr, [y * y for y in dy], r, step, 2)
        stiff_here = get(s, r, step)
        inverse = [lax.rsqrt(jnp.maximum(x, 0.05)) for x in stiff_here]
        put(rq, inverse, r, step)
        put(q, [x * y for x, y in zip(stiff_here, inverse)], r, step)

    def three_rows(ks):
        def body(r, step):
            for k in ks:
                put(p3, add(*(get(pr, r + d, step, k) for d in (-1, 0, 1))), r, step, k)

        return body

    kept = jnp.where(has_next, jnp.float32(1.0), jnp.float32(0.0))
    cells = float((2 * RADIUS + 1) ** 2)

    def window(low, high, ks, factor):
        scale = kept * (factor / cells)

        def body(r, step):
            parts = []
            for k in ks:
                x = jnp.concatenate(add(*(get(p3, r + d, step, k) for d in (-3, 0, 3))), axis=1)
                coarse = x.astype(jnp.bfloat16)
                parts += [coarse, (x - coarse.astype(jnp.float32)).astype(jnp.bfloat16)]
            y = jnp.dot(
                jnp.concatenate(parts, axis=0), band[...], preferred_element_type=jnp.float32
            )
            for i, k in enumerate(ks):
                z = y[2 * i * step:(2 * i + 1) * step] + y[(2 * i + 1) * step:(2 * i + 2) * step]
                value = [z[:, columns_of(j)] * scale for j in range(nb)]
                put(tt, value, r, step, k)
                if EDGE <= r < end:
                    for j in range(nw):
                        tensor_out[k, 0, pl.ds(r - EDGE, step), columns(j)] = value[j]

        if low < EDGE:
            body(low, EDGE - low)
        blocks(max(low, EDGE), min(high, end), WIN, body)
        if high > end:
            body(end, high - end)


    settled = 8 * (SWEEPS - 1)

    def span(c, ahead, margin):
        low = first + margin if c == 0 else bounds[c] + ahead
        high = last - margin if c == chunks - 1 else min(bounds[c + 1] + ahead, last - margin)
        return min(low, high), high

    def beyond_grid(there, at):
        @pl.when(jnp.logical_not(there))
        def _():
            for ref in (gx, gy):
                clear(ref.at[:, at])
            clear(pr.at[pl.ds(0, 3), :, at])

    def own_products(c):
        low, high = span(c, settled + 16, 0)
        blocks(low, high, GRAD, gradient)
        if c == 0:
            beyond_grid(has_up, top)
        if low < last == high:
            beyond_grid(has_down, bottom)
        blocks(*span(c, settled + 8, 0), 16, three_rows((0, 1, 2)))
        window(*span(c, settled, 8), (0, 1, 2), 0.25)

    def change(r, step):
        moved = [x - y for x, y in zip(get(b, r, step), get(a, r, step))]
        put(pr, [x * y for x, y in zip(get(gx, r, step), moved)], r, step, 3)
        put(pr, [x * y for x, y in zip(get(gy, r, step), moved)], r, step, 4)

    def near(source, r, step, part, count):
        mid = get(source, r, step, part)
        lane = lanes_of(step)
        return add(
            get(source, r - 1, step, part), get(source, r + 1, step, part),
            shifted(mid, 1, lane), shifted(mid, -1, lane),
        )[:count]

    def relaxed(source, r, step, start, count):
        nx, ny = (near(source, r, step, part, count) for part in range(2))
        xx, xy, yy = (get(ref, r, step)[:count] for ref in (ca, cb, cc))
        x, y = start
        return (
            [x[k] + (xx[k] * nx[k] - xy[k] * ny[k]) for k in range(count)],
            [y[k] + (yy[k] * ny[k] - xy[k] * nx[k]) for k in range(count)],
        )

    def setup(r, step):
        lane = lanes_of(step)
        xx, xy, yy, xt, yt = (get(tt, r, step, k) for k in range(5))
        mid = get(q, r, step)
        around = add(
            get(q, r - 1, step), get(q, r + 1, step), shifted(mid, 1, lane), shifted(mid, -1, lane)
        )
        at = pl.ds(r, step)
        for k in range(nb):
            diag = mid[k] * around[k] + 2.0 * COUPLING
            one, two = xx[k] + diag, yy[k] + diag
            inverse = mid[k] / (one * two - xy[k] * xy[k])
            xa, xb, xc = two * inverse, xy[k] * inverse, one * inverse
            g0[0, k, at, :] = xb * yt[k] - xa * xt[k]
            g0[1, k, at, :] = xb * xt[k] - xc * yt[k]
            for ref, value in ((ca, xa), (cb, xb), (cc, xc)):
                ref[k, at, :] = value * mid[k]

    def sweep(source, start, target, unscaled=None):
        def body(r, step):
            new = relaxed(
                source, r, step, [get(start, r, step, part) for part in range(2)], nb
            )
            here = get(rq, r, step) if unscaled is not None else None
            for part in range(2):
                if target is not None:
                    put(target, new[part], r, step, part)
                if unscaled is not None:
                    put(unscaled, [x * y for x, y in zip(new[part], here)], r, step, part)

        return body

    def stages(c, bodies, lead, ends):
        for k, body in enumerate(bodies):
            margin = ends[k == len(bodies) - 1]
            low, high = span(c, 8 * (lead - k), margin)
            blocks(max(low, first + margin), high, SWEEP, body)

    first_round = [setup, sweep(g0, g0, g1), sweep(g1, g0, g2), sweep(g2, g0, g3, field)]

    to_next, to_prev = [], []
    for c in range(min(LEAD, chunks)):
        own_products(c)
    for c in range(chunks):
        when_got(has_next, tile_b[c])
        if c == 0:
            for there, copy in forward_rows + forward_cols:
                when_got(has_next & there, [copy])
            unpack(b, next_left, next_right, next_corner, 0)
        blocks(*span(c, settled + 16, 0), 32, change)
        blocks(*span(c, settled + 8, 0), 16, three_rows((3, 4)))
        window(*span(c, settled, 8), (3, 4), 0.5)
        stages(c, first_round, SWEEPS - 1, (8, 8))
        low, high = bounds[c], bounds[c + 1]
        folded = pl.ds((low - first) // FOLD, (high - low) // FOLD)
        pack_rim(field, rim, low, high, first, nw)
        rows_sent = pl.ds(max(low, first + 8), min(high, last - 8) - max(low, first + 8))

        def moves(rims, mains, device, way):
            pairs = (
                (rim.at[folded], rims.at[folded]),
                (field.at[:, main, rows_sent], mains.at[:, main, rows_sent]),
            )
            return [
                pltpu.make_async_remote_copy(
                    src_ref=src, dst_ref=dst, send_sem=chunk_send.at[way + i, c],
                    recv_sem=chunk_recv.at[way + i, c], device_id=device, device_id_type=MESH,
                )
                for i, (src, dst) in enumerate(pairs)
            ]

        to_next.append(moves(rim_before, main_before, next_id, 0))
        to_prev.append(moves(rim_after, main_after, prev_id, 2))
        when_start(has_next, to_next[c])
        when_start(has_prev, to_prev[c])
        if c + LEAD < chunks:
            own_products(c + LEAD)

    def coupled(r, step):
        at = pl.ds(r, step)

        def beside(part, ref):
            return [
                main_before[part, k, at, :] + main_after[part, k, at, :] for k in range(nw)
            ] + [ref[nw, at, :]]

        x, y = beside(0, gx), beside(1, gy)
        xx, xy, yy = (get(ref, r, step) for ref in (ca, cb, cc))
        weight = [v * COUPLING for v in get(rq, r, step)]
        old = [get(g0, r, step, part) for part in range(2)]
        start = (
            [old[0][k] + weight[k] * (xx[k] * x[k] - xy[k] * y[k]) for k in range(nb)],
            [old[1][k] + weight[k] * (yy[k] * y[k] - xy[k] * x[k]) for k in range(nb)],
        )
        new = relaxed(g3, r, step, start, nb)
        for part in range(2):
            put(kk, start[part], r, step, part)
            put(g1, new[part], r, step, part)

    def final(r, step):
        start = [get(kk, r, step, part) for part in range(2)]
        new = relaxed(g4, r, step, start, nw)
        here = get(rq, r, step)
        for part in range(2):
            for k in range(nw):
                field_out[part, 0, pl.ds(r - EDGE, step), columns(k)] = new[part][k] * here[k]

    second_round = [coupled, sweep(g1, kk, g2), sweep(g2, kk, g4), final]
    for c in range(chunks):
        when_got(has_prev, to_next[c])
        when_got(has_next, to_prev[c])
        low, high = bounds[c], bounds[c + 1]
        size = (high - low) // FOLD
        folded = pl.ds((low - first) // FOLD, size)
        both = rim_before[folded, :] + rim_after[folded, :]
        lane = lanes_of(size)
        for j in range(FOLD):
            for k, ref in enumerate((gx, gy)):
                slot = (2 * j + k) * SLOT
                head = jnp.where(lane < 8, lane_roll(both, -slot), 0.0)
                tail = lane_roll(both, LANES - 16 - slot)
                ref[nw, pl.ds(low + j * size, size), :] = jnp.where(
                    lane >= LANES - 8, tail, head
                )
        stages(c, second_round, 0, (8, 16))

    for c in range(chunks):
        when_sent(has_next, to_next[c])
        when_sent(has_prev, to_prev[c])
    when_sent(has_up, up)
    when_sent(has_down, down)
    when_sent(has_right, [col_right])
    when_sent(has_left, [col_left])
    for (there, _device), copy in zip(corners, to_corner):
        when_sent(there, [copy])
    when_sent(has_prev, sum(tile_b, []))
    for there, copy in forward_rows + forward_cols:
        when_sent(has_prev & there, [copy])


def pack_rim(field, rim, low, high, first, nw):
    size = (high - low) // FOLD
    lane = lax.broadcasted_iota(jnp.int32, (size, LANES), 1)
    out = jnp.zeros((size, LANES), jnp.float32)
    for j in range(FOLD):
        at = pl.ds(low + j * size, size)
        for k in range(2):
            slot = (2 * j + k) * SLOT
            block = field[k, nw, at, :]
            head, tail = lane_roll(block, slot), lane_roll(block, slot + SLOT)
            out = jnp.where((lane >= slot) & (lane < slot + 8), head, out)
            out = jnp.where((lane >= slot + 8) & (lane < slot + 16), tail, out)
    rim[pl.ds((low - first) // FOLD, size), :] = out


def store(tensor, field, tensor_out, field_out, sem):
    pairs = ((tensor, tensor_out), (field, field_out))
    copies = [pltpu.make_async_copy(src, dst, sem.at[i]) for i, (src, dst) in enumerate(pairs)]
    for copy in copies:
        copy.start()
    for copy in copies:
        copy.wait()


def local(counts, images, stiffness):
    _, rows, width = images.shape
    nw = width // LANES
    nb = nw + 1
    total = rows + 2 * EDGE
    f32 = jnp.float32
    plane = pltpu.VMEM((nb, total, LANES), f32)
    five = pltpu.VMEM((5, nb, total, LANES), f32)
    pair = pltpu.VMEM((2, nb, total, LANES), f32)
    packet = pltpu.VMEM(((rows + 2 * HALO) // FOLD, LANES), f32)
    mains = pltpu.VMEM((2, nw, total, LANES), f32)
    chunks = len(bounds_of(rows, 0)) - 1
    results = pl.pallas_call(
        functools.partial(kernel, counts),
        out_shape=(
            jax.ShapeDtypeStruct((5, 1, rows, width), f32),
            jax.ShapeDtypeStruct((2, 1, rows, width), f32),
        ),
        in_specs=[pl.BlockSpec(memory_space=pltpu.HBM)] * 2,
        out_specs=[pl.BlockSpec(memory_space=pltpu.VMEM)] * 2,
        scratch_shapes=[plane] * 7
        + [five] * 3
        + [plane] * 3
        + [pair] * 7
        + [packet] * 6
        + [pltpu.VMEM((4, HALO, LANES), f32)] * 2
        + [packet] * 3
        + [mains] * 2
        + [pltpu.VMEM((nb * LANES, nb * LANES), jnp.bfloat16)]
        + [
            pltpu.SemaphoreType.DMA((2, nw)),
            pltpu.SemaphoreType.DMA((KINDS, nw)),
            pltpu.SemaphoreType.DMA((KINDS, nw)),
            pltpu.SemaphoreType.DMA((4, chunks)),
            pltpu.SemaphoreType.DMA((4, chunks)),
            pltpu.SemaphoreType.DMA((chunks, nw)),
            pltpu.SemaphoreType.DMA((chunks, nw)),
        ],
        compiler_params=pltpu.CompilerParams(
            collective_id=0, has_side_effects=True, vmem_limit_bytes=48 * 1024 * 1024
        ),
    )(*(pltpu.with_memory_space_constraint(x, pltpu.HBM) for x in (images, stiffness)))
    return pl.pallas_call(
        store,
        out_shape=tuple(jax.ShapeDtypeStruct(x.shape, f32) for x in results),
        in_specs=[pl.BlockSpec(memory_space=pltpu.VMEM)] * 2,
        out_specs=[pl.BlockSpec(memory_space=pltpu.HBM)] * 2,
        scratch_shapes=[pltpu.SemaphoreType.DMA((2,))],
        compiler_params=pltpu.CompilerParams(vmem_limit_bytes=4 * 1024 * 1024),
    )(*results)


def solution(mesh):
    counts = tuple(mesh.shape[name] for name in ("sec", "row", "col"))
    spec = P("sec", "row", "col")
    out = P(None, "sec", "row", "col")
    return jax.shard_map(
        functools.partial(local, counts), mesh=mesh, in_specs=(spec, spec),
        out_specs=(out, out), check_vma=False,
    )
```

```python
import functools

import jax
import jax.numpy as jnp
from jax import lax
from jax.experimental import pallas as pl
from jax.experimental.pallas import tpu as pltpu
from jax.sharding import PartitionSpec as P

RADIUS = 4
SWEEPS = 4
ROUNDS = 2
COUPLING = 0.25
MESH = pl.DeviceIdType.MESH

LANES = 128
HALO = 16
EDGE = HALO + 8
LEAD = 9
GRAD = 16
WIN = 128
SWEEP = 16
EARLY = 2
SLOT = 16
CHUNK = 64
SHORT = 64
FOLD = LANES // (2 * SLOT)

(
    TILE_B, ROW_A_UP, ROW_A_DOWN, ROW_S_UP, ROW_S_DOWN, FWD_TOP, FWD_BOTTOM, COL_RIGHT, COL_LEFT,
    FWD_RIGHT, FWD_LEFT, CORNER, _, _, _, FWD_CORNER, _, _, _,
) = range(19)
KINDS = 19


def bounds_of(rows, first):
    last = first + rows + 2 * HALO
    inside = list(range(first + SHORT, last - SHORT - CHUNK // 2, CHUNK))
    return [first] + inside + [last - SHORT, last]


def lane_roll(x, shift):
    return pltpu.roll(x, shift % x.shape[1], 1)


def columns_of(k):
    return slice(k * LANES, (k + 1) * LANES)


def shifted(blocks, shift, lane):
    rolled = [lane_roll(x, shift) for x in blocks]
    out = []
    for k, here in enumerate(rolled):
        if shift > 0:
            out.append(jnp.where(lane < shift, rolled[k - 1], here))
        else:
            out.append(jnp.where(lane >= LANES + shift, rolled[(k + 1) % len(rolled)], here))
    return out


def add(*terms):
    return [sum(xs[1:], xs[0]) for xs in zip(*terms)]


def kernel(
    counts, images, stiff, tensor_out, field_out,
    a, b, s, q, rq, gx, gy, pr, p3, tt, ca, cb, cc, g0, g1, g2, g3, g4, kk, field,
    send_right, send_left, got_left, got_right, next_left, next_right, corner, next_corner,
    rim, rim_before, rim_after, main_before, main_after, band,
    local_sem, send_sem, recv_sem, chunk_send, chunk_recv, tile_send, tile_recv,
):
    sec, row, col = (lax.axis_index(name) for name in ("sec", "row", "col"))
    n_sec, n_row, n_col = counts
    rows, width = images.shape[1], images.shape[2]
    nb, total, _ = a.shape
    nw = nb - 1
    has_prev, has_next = sec > 0, sec < n_sec - 1
    has_up, has_down = row > 0, row < n_row - 1
    has_left, has_right = col > 0, col < n_col - 1
    sides = (
        (has_prev, (sec - 1, row, col)), (has_next, (sec + 1, row, col)),
        (has_up, (sec, row - 1, col)), (has_down, (sec, row + 1, col)),
        (has_left, (sec, row, col - 1)), (has_right, (sec, row, col + 1)),
    )
    prev_id, next_id, up_id, down_id, left_id, right_id = (side[1] for side in sides)
    corners = tuple(
        (there_row & there_col, (sec, row + step_row, col + step_col))
        for there_row, step_row in ((has_up, -1), (has_down, 1))
        for there_col, step_col in ((has_left, -1), (has_right, 1))
    )
    end = EDGE + rows
    first, last = EDGE - HALO, end + HALO
    inner = pl.ds(EDGE, rows)
    main = pl.ds(0, nw)
    top, bottom = pl.ds(EDGE - HALO, HALO), pl.ds(end, HALO)
    piece = (last - first) // FOLD

    def remote(src, dst, k, device, part=0):
        return pltpu.make_async_remote_copy(
            src_ref=src, dst_ref=dst, send_sem=send_sem.at[k, part],
            recv_sem=recv_sem.at[k, part], device_id=device, device_id_type=MESH,
        )

    def columns(k):
        return pl.ds(k * LANES, LANES)

    loads = [
        pltpu.make_async_copy(src.at[0, :, columns(k)], dst.at[k, inner], local_sem.at[i, k])
        for i, (src, dst) in enumerate(((images, a), (stiff, s)))
        for k in range(nw)
    ]
    for copy in loads:
        copy.start()
    barrier = pltpu.get_barrier_semaphore()
    for there, device in sides + corners:
        @pl.when(there)
        def _():
            pl.semaphore_signal(barrier, inc=1, device_id=device, device_id_type=MESH)

    def clear(ref):
        ref[...] = jnp.zeros(ref.shape, jnp.float32)

    @pl.when(jnp.logical_not(has_up))
    def _():
        clear(a.at[main, top])
        clear(b.at[main, top])
        clear(s.at[main, top])

    @pl.when(jnp.logical_not(has_down))
    def _():
        clear(a.at[main, bottom])
        clear(b.at[main, bottom])
        clear(s.at[main, bottom])

    @pl.when(jnp.logical_not(has_left))
    def _():
        clear(got_left)
        clear(next_left)

    @pl.when(jnp.logical_not(has_right))
    def _():
        clear(got_right)
        clear(next_right)

    for i, (there, _device) in enumerate(corners):
        @pl.when(jnp.logical_not(there))
        def _():
            clear(corner.at[i])
            clear(next_corner.at[i])

    @pl.when(jnp.logical_not(has_next))
    def _():
        clear(b)
        clear(next_corner)
        clear(next_left)
        clear(next_right)
        clear(rim_after)
        clear(main_after)

    @pl.when(jnp.logical_not(has_prev))
    def _():
        clear(rim_before)
        clear(main_before)

    src = lax.broadcasted_iota(jnp.int32, (nb * LANES, nb * LANES), 0)
    dst = lax.broadcasted_iota(jnp.int32, (nb * LANES, nb * LANES), 1)
    fold_at = nw * LANES + LANES // 2
    src = jnp.where(src < fold_at, src, src - nb * LANES)
    dst = jnp.where(dst < fold_at, dst, dst - nb * LANES)
    band[...] = jnp.where(jnp.abs(src - dst) <= RADIUS, 1.0, 0.0).astype(jnp.bfloat16)

    def lanes_of(count):
        return lax.broadcasted_iota(jnp.int32, (count, LANES), 1)

    def packed(to, block, at):
        for low, high, folds in (
            (0, HALO, range(1, FOLD)), (HALO, piece - HALO, range(FOLD)),
            (piece - HALO, piece, range(FOLD - 1)),
        ):
            lane = lanes_of(high - low)
            out = jnp.zeros((high - low, LANES), jnp.float32)
            for j in folds:
                span = pl.ds(first + j * piece + low, high - low)
                for k, ref in enumerate((a, s)):
                    slot = (2 * j + k) * SLOT
                    moved = lane_roll(ref[block, span, :], slot - at)
                    out = jnp.where((lane >= slot) & (lane < slot + SLOT), moved, out)
            to[pl.ds(low, high - low), :] = out

    for copy in loads:
        copy.wait()

    @pl.when(has_right)
    def _():
        packed(send_right, nw - 1, LANES - SLOT)

    @pl.when(has_left)
    def _():
        packed(send_left, 0, 0)

    pl.semaphore_wait(barrier, sum(jnp.where(there, 1, 0) for there, _device in sides + corners))

    def by_block(src, at, dst, to, k, device):
        return [
            remote(src.at[0, at, columns(p)], dst.at[p, to], k, device, p) for p in range(nw)
        ]

    low, high = pl.ds(0, HALO), pl.ds(rows - HALO, HALO)
    bounds = bounds_of(rows, first)
    chunks = len(bounds) - 1
    ahead = 8 * (SWEEPS + 1)
    cuts = [0] + [min(high + ahead - EDGE, rows) for high in bounds[1:-1]] + [rows]

    def tile_piece(c):
        if cuts[c] == cuts[c + 1]:
            return []
        at, to = pl.ds(cuts[c], cuts[c + 1] - cuts[c]), pl.ds(EDGE + cuts[c], cuts[c + 1] - cuts[c])
        return [
            pltpu.make_async_remote_copy(
                src_ref=images.at[0, at, columns(p)], dst_ref=b.at[p, to],
                send_sem=tile_send.at[c, p], recv_sem=tile_recv.at[c, p],
                device_id=prev_id, device_id_type=MESH,
            )
            for p in range(nw)
        ]

    tile_b = [tile_piece(c) for c in range(chunks)]
    near = HALO // 2
    up = by_block(stiff, pl.ds(0, near), s, pl.ds(end, near), ROW_S_UP, up_id)
    up += by_block(images, low, a, bottom, ROW_A_UP, up_id)
    down = by_block(
        stiff, pl.ds(rows - near, near), s, pl.ds(EDGE - near, near), ROW_S_DOWN, down_id
    )
    down += by_block(images, high, a, top, ROW_A_DOWN, down_id)
    col_right = remote(send_right, got_left, COL_RIGHT, right_id)
    col_left = remote(send_left, got_right, COL_LEFT, left_id)
    forward_rows = [
        (has_up, remote(a.at[main, top], b.at[main, top], FWD_TOP, prev_id)),
        (has_down, remote(a.at[main, bottom], b.at[main, bottom], FWD_BOTTOM, prev_id)),
    ]
    forward_cols = [
        (has_left, remote(got_left, next_left, FWD_LEFT, prev_id)),
        (has_right, remote(got_right, next_right, FWD_RIGHT, prev_id)),
    ] + [
        (there, remote(corner.at[i], next_corner.at[i], FWD_CORNER + i, prev_id))
        for i, (there, _device) in enumerate(corners)
    ]
    head, tail = pl.ds(HALO, HALO), pl.ds(piece - 2 * HALO, HALO)
    to_corner = [
        remote(sent.at[at], corner.at[3 - i], CORNER + i, corners[i][1])
        for i, (sent, at) in enumerate(
            ((send_left, head), (send_right, head), (send_left, tail), (send_right, tail))
        )
    ]

    def when_start(there, copies):
        @pl.when(there)
        def _():
            for copy in copies:
                copy.start()

    def when_got(there, copies):
        @pl.when(there)
        def _():
            for copy in copies:
                copy.wait_recv()

    def when_sent(there, copies):
        @pl.when(there)
        def _():
            for copy in copies:
                copy.wait_send()

    for (there, _device), copy in zip(corners, to_corner):
        when_start(there, [copy])
    @pl.when(has_right)
    def _():
        col_right.start()

    @pl.when(has_left)
    def _():
        col_left.start()

    when_start(has_up, up)
    when_start(has_down, down)
    when_start(has_prev, sum(tile_b[:EARLY], []))
    def rim_of(left, right, j, k):
        lane = lanes_of(right.shape[0])
        slot = (2 * j + k) * SLOT
        from_right = jnp.where(lane < SLOT, lane_roll(right, -slot), 0.0)
        return jnp.where(lane >= LANES - SLOT, lane_roll(left, LANES - SLOT - slot), from_right)

    def unpack(ref, left, right, around, k):
        for j in range(FOLD):
            low = HALO if j == 0 else 0
            high = piece - HALO if j == FOLD - 1 else piece
            at = pl.ds(low, high - low)
            ref[nw, pl.ds(first + j * piece + low, high - low), :] = rim_of(
                left[at, :], right[at, :], j, k
            )
        ref[nw, top, :] = rim_of(around[0], around[1], FOLD - 1, k)
        ref[nw, bottom, :] = rim_of(around[2], around[3], 0, k)

    when_got(has_left, [col_right])
    when_got(has_right, [col_left])
    for there, copy in forward_cols[:2]:
        when_start(has_prev & there, [copy])
    when_got(has_up, down)
    when_got(has_down, up)
    for there, copy in forward_rows:
        when_start(has_prev & there, [copy])
    for (there, _device), copy in zip(corners, reversed(to_corner)):
        when_got(there, [copy])
    for there, copy in forward_cols[2:]:
        when_start(has_prev & there, [copy])
    when_start(has_prev, sum(tile_b[EARLY:], []))
    unpack(a, got_left, got_right, corner, 0)
    unpack(s, got_left, got_right, corner, 1)

    def get(ref, r, step, *lead):
        return [ref[(*lead, k, pl.ds(r, step), slice(None))] for k in range(nb)]

    def put(ref, values, r, step, *lead):
        for k, value in enumerate(values):
            ref[(*lead, k, pl.ds(r, step), slice(None))] = value

    def blocks(low, high, step, body):
        for r in range(low, high, step):
            body(r, min(step, high - r))

    def gradient(r, step):
        lane = lanes_of(step)
        rim_ok = ((lane < LANES // 2) & has_right) | ((lane >= LANES // 2) & has_left)
        mid = get(a, r, step)
        after, before = shifted(mid, -1, lane), shifted(mid, 1, lane)
        under, over = get(a, r + 1, step), get(a, r - 1, step)
        dx = [x - y for x, y in zip(after, before)]
        dy = [x - y for x, y in zip(under, over)]
        dx[nw], dy[nw] = jnp.where(rim_ok, dx[nw], 0.0), jnp.where(rim_ok, dy[nw], 0.0)
        put(gx, dx, r, step)
        put(gy, dy, r, step)
        put(pr, [x * x for x in dx], r, step, 0)
        put(pr, [x * y for x, y in zip(dx, dy)], r, step, 1)
        put(pr, [y * y for y in dy], r, step, 2)
        stiff_here = get(s, r, step)
        inverse = [lax.rsqrt(jnp.maximum(x, 0.05)) for x in stiff_here]
        put(rq, inverse, r, step)
        put(q, [x * y for x, y in zip(stiff_here, inverse)], r, step)

    def three_rows(ks):
        def body(r, step):
            for k in ks:
                put(p3, add(*(get(pr, r + d, step, k) for d in (-1, 0, 1))), r, step, k)

        return body

    kept = jnp.where(has_next, jnp.float32(1.0), jnp.float32(0.0))
    cells = float((2 * RADIUS + 1) ** 2)

    def window(low, high, ks, factor):
        scale = kept * (factor / cells)

        def body(r, step):
            parts = []
            for k in ks:
                x = jnp.concatenate(add(*(get(p3, r + d, step, k) for d in (-3, 0, 3))), axis=1)
                coarse = x.astype(jnp.bfloat16)
                parts += [coarse, (x - coarse.astype(jnp.float32)).astype(jnp.bfloat16)]
            y = jnp.dot(
                jnp.concatenate(parts, axis=0), band[...], preferred_element_type=jnp.float32
            )
            for i, k in enumerate(ks):
                z = y[2 * i * step:(2 * i + 1) * step] + y[(2 * i + 1) * step:(2 * i + 2) * step]
                value = [z[:, columns_of(j)] * scale for j in range(nb)]
                put(tt, value, r, step, k)
                if EDGE <= r < end:
                    for j in range(nw):
                        tensor_out[k, 0, pl.ds(r - EDGE, step), columns(j)] = value[j]

        if low < EDGE:
            body(low, EDGE - low)
        blocks(max(low, EDGE), min(high, end), WIN, body)
        if high > end:
            body(end, high - end)


    settled = 8 * (SWEEPS - 1)

    def span(c, ahead, margin):
        low = first + margin if c == 0 else bounds[c] + ahead
        high = last - margin if c == chunks - 1 else min(bounds[c + 1] + ahead, last - margin)
        return min(low, high), high

    def beyond_grid(there, at):
        @pl.when(jnp.logical_not(there))
        def _():
            for ref in (gx, gy):
                clear(ref.at[:, at])
            clear(pr.at[pl.ds(0, 3), :, at])

    def own_products(c):
        low, high = span(c, settled + 16, 0)
        blocks(low, high, GRAD, gradient)
        if c == 0:
            beyond_grid(has_up, top)
        if low < last == high:
            beyond_grid(has_down, bottom)
        blocks(*span(c, settled + 8, 0), 16, three_rows((0, 1, 2)))
        window(*span(c, settled, 8), (0, 1, 2), 0.25)

    def change(r, step):
        moved = [x - y for x, y in zip(get(b, r, step), get(a, r, step))]
        put(pr, [x * y for x, y in zip(get(gx, r, step), moved)], r, step, 3)
        put(pr, [x * y for x, y in zip(get(gy, r, step), moved)], r, step, 4)

    def near(source, r, step, part, count):
        mid = get(source, r, step, part)
        lane = lanes_of(step)
        return add(
            get(source, r - 1, step, part), get(source, r + 1, step, part),
            shifted(mid, 1, lane), shifted(mid, -1, lane),
        )[:count]

    def relaxed(source, r, step, start, count):
        nx, ny = (near(source, r, step, part, count) for part in range(2))
        xx, xy, yy = (get(ref, r, step)[:count] for ref in (ca, cb, cc))
        x, y = start
        return (
            [x[k] + (xx[k] * nx[k] - xy[k] * ny[k]) for k in range(count)],
            [y[k] + (yy[k] * ny[k] - xy[k] * nx[k]) for k in range(count)],
        )

    def setup(r, step):
        lane = lanes_of(step)
        xx, xy, yy, xt, yt = (get(tt, r, step, k) for k in range(5))
        mid = get(q, r, step)
        around = add(
            get(q, r - 1, step), get(q, r + 1, step), shifted(mid, 1, lane), shifted(mid, -1, lane)
        )
        at = pl.ds(r, step)
        for k in range(nb):
            diag = mid[k] * around[k] + 2.0 * COUPLING
            one, two = xx[k] + diag, yy[k] + diag
            inverse = mid[k] / (one * two - xy[k] * xy[k])
            xa, xb, xc = two * inverse, xy[k] * inverse, one * inverse
            g0[0, k, at, :] = xb * yt[k] - xa * xt[k]
            g0[1, k, at, :] = xb * xt[k] - xc * yt[k]
            for ref, value in ((ca, xa), (cb, xb), (cc, xc)):
                ref[k, at, :] = value * mid[k]

    def sweep(source, start, target, unscaled=None):
        def body(r, step):
            new = relaxed(
                source, r, step, [get(start, r, step, part) for part in range(2)], nb
            )
            here = get(rq, r, step) if unscaled is not None else None
            for part in range(2):
                if target is not None:
                    put(target, new[part], r, step, part)
                if unscaled is not None:
                    put(unscaled, [x * y for x, y in zip(new[part], here)], r, step, part)

        return body

    def stages(c, bodies, lead, ends):
        for k, body in enumerate(bodies):
            margin = ends[k == len(bodies) - 1]
            low, high = span(c, 8 * (lead - k), margin)
            blocks(max(low, first + margin), high, SWEEP, body)

    first_round = [setup, sweep(g0, g0, g1), sweep(g1, g0, g2), sweep(g2, g0, g3, field)]

    to_next, to_prev = [], []
    for c in range(min(LEAD, chunks)):
        own_products(c)
    for c in range(chunks):
        when_got(has_next, tile_b[c])
        if c == 0:
            for there, copy in forward_rows + forward_cols:
                when_got(has_next & there, [copy])
            unpack(b, next_left, next_right, next_corner, 0)
        blocks(*span(c, settled + 16, 0), 32, change)
        blocks(*span(c, settled + 8, 0), 16, three_rows((3, 4)))
        window(*span(c, settled, 8), (3, 4), 0.5)
        stages(c, first_round, SWEEPS - 1, (8, 8))
        low, high = bounds[c], bounds[c + 1]
        folded = pl.ds((low - first) // FOLD, (high - low) // FOLD)
        pack_rim(field, rim, low, high, first, nw)
        rows_sent = pl.ds(max(low, first + 8), min(high, last - 8) - max(low, first + 8))

        def moves(rims, mains, device, way):
            pairs = (
                (rim.at[folded], rims.at[folded]),
                (field.at[:, main, rows_sent], mains.at[:, main, rows_sent]),
            )
            return [
                pltpu.make_async_remote_copy(
                    src_ref=src, dst_ref=dst, send_sem=chunk_send.at[way + i, c],
                    recv_sem=chunk_recv.at[way + i, c], device_id=device, device_id_type=MESH,
                )
                for i, (src, dst) in enumerate(pairs)
            ]

        to_next.append(moves(rim_before, main_before, next_id, 0))
        to_prev.append(moves(rim_after, main_after, prev_id, 2))
        when_start(has_next, to_next[c])
        when_start(has_prev, to_prev[c])
        if c + LEAD < chunks:
            own_products(c + LEAD)

    def coupled(r, step):
        at = pl.ds(r, step)

        def beside(part, ref):
            return [
                main_before[part, k, at, :] + main_after[part, k, at, :] for k in range(nw)
            ] + [ref[nw, at, :]]

        x, y = beside(0, gx), beside(1, gy)
        xx, xy, yy = (get(ref, r, step) for ref in (ca, cb, cc))
        weight = [v * COUPLING for v in get(rq, r, step)]
        old = [get(g0, r, step, part) for part in range(2)]
        start = (
            [old[0][k] + weight[k] * (xx[k] * x[k] - xy[k] * y[k]) for k in range(nb)],
            [old[1][k] + weight[k] * (yy[k] * y[k] - xy[k] * x[k]) for k in range(nb)],
        )
        new = relaxed(g3, r, step, start, nb)
        for part in range(2):
            put(kk, start[part], r, step, part)
            put(g1, new[part], r, step, part)

    def final(r, step):
        start = [get(kk, r, step, part) for part in range(2)]
        new = relaxed(g4, r, step, start, nw)
        here = get(rq, r, step)
        for part in range(2):
            for k in range(nw):
                field_out[part, 0, pl.ds(r - EDGE, step), columns(k)] = new[part][k] * here[k]

    second_round = [coupled, sweep(g1, kk, g2), sweep(g2, kk, g4), final]
    for c in range(chunks):
        when_got(has_prev, to_next[c])
        when_got(has_next, to_prev[c])
        low, high = bounds[c], bounds[c + 1]
        size = (high - low) // FOLD
        folded = pl.ds((low - first) // FOLD, size)
        both = rim_before[folded, :] + rim_after[folded, :]
        lane = lanes_of(size)
        for j in range(FOLD):
            for k, ref in enumerate((gx, gy)):
                slot = (2 * j + k) * SLOT
                head = jnp.where(lane < 8, lane_roll(both, -slot), 0.0)
                tail = lane_roll(both, LANES - 16 - slot)
                ref[nw, pl.ds(low + j * size, size), :] = jnp.where(
                    lane >= LANES - 8, tail, head
                )
        stages(c, second_round, 0, (8, 16))

    for c in range(chunks):
        when_sent(has_next, to_next[c])
        when_sent(has_prev, to_prev[c])
    when_sent(has_up, up)
    when_sent(has_down, down)
    when_sent(has_right, [col_right])
    when_sent(has_left, [col_left])
    for (there, _device), copy in zip(corners, to_corner):
        when_sent(there, [copy])
    when_sent(has_prev, sum(tile_b, []))
    for there, copy in forward_rows + forward_cols:
        when_sent(has_prev & there, [copy])


def pack_rim(field, rim, low, high, first, nw):
    size = (high - low) // FOLD
    lane = lax.broadcasted_iota(jnp.int32, (size, LANES), 1)
    out = jnp.zeros((size, LANES), jnp.float32)
    for j in range(FOLD):
        at = pl.ds(low + j * size, size)
        for k in range(2):
            slot = (2 * j + k) * SLOT
            block = field[k, nw, at, :]
            head, tail = lane_roll(block, slot), lane_roll(block, slot + SLOT)
            out = jnp.where((lane >= slot) & (lane < slot + 8), head, out)
            out = jnp.where((lane >= slot + 8) & (lane < slot + 16), tail, out)
    rim[pl.ds((low - first) // FOLD, size), :] = out


def store(tensor, field, tensor_out, field_out, sem):
    pairs = ((tensor, tensor_out), (field, field_out))
    copies = [pltpu.make_async_copy(src, dst, sem.at[i]) for i, (src, dst) in enumerate(pairs)]
    for copy in copies:
        copy.start()
    for copy in copies:
        copy.wait()


def local(counts, images, stiffness):
    _, rows, width = images.shape
    nw = width // LANES
    nb = nw + 1
    total = rows + 2 * EDGE
    f32 = jnp.float32
    plane = pltpu.VMEM((nb, total, LANES), f32)
    five = pltpu.VMEM((5, nb, total, LANES), f32)
    pair = pltpu.VMEM((2, nb, total, LANES), f32)
    packet = pltpu.VMEM(((rows + 2 * HALO) // FOLD, LANES), f32)
    mains = pltpu.VMEM((2, nw, total, LANES), f32)
    chunks = len(bounds_of(rows, 0)) - 1
    results = pl.pallas_call(
        functools.partial(kernel, counts),
        out_shape=(
            jax.ShapeDtypeStruct((5, 1, rows, width), f32),
            jax.ShapeDtypeStruct((2, 1, rows, width), f32),
        ),
        in_specs=[pl.BlockSpec(memory_space=pltpu.HBM)] * 2,
        out_specs=[pl.BlockSpec(memory_space=pltpu.VMEM)] * 2,
        scratch_shapes=[plane] * 7
        + [five] * 3
        + [plane] * 3
        + [pair] * 7
        + [packet] * 6
        + [pltpu.VMEM((4, HALO, LANES), f32)] * 2
        + [packet] * 3
        + [mains] * 2
        + [pltpu.VMEM((nb * LANES, nb * LANES), jnp.bfloat16)]
        + [
            pltpu.SemaphoreType.DMA((2, nw)),
            pltpu.SemaphoreType.DMA((KINDS, nw)),
            pltpu.SemaphoreType.DMA((KINDS, nw)),
            pltpu.SemaphoreType.DMA((4, chunks)),
            pltpu.SemaphoreType.DMA((4, chunks)),
            pltpu.SemaphoreType.DMA((chunks, nw)),
            pltpu.SemaphoreType.DMA((chunks, nw)),
        ],
        compiler_params=pltpu.CompilerParams(
            collective_id=0, has_side_effects=True, vmem_limit_bytes=48 * 1024 * 1024
        ),
    )(*(pltpu.with_memory_space_constraint(x, pltpu.HBM) for x in (images, stiffness)))
    return pl.pallas_call(
        store,
        out_shape=tuple(jax.ShapeDtypeStruct(x.shape, f32) for x in results),
        in_specs=[pl.BlockSpec(memory_space=pltpu.VMEM)] * 2,
        out_specs=[pl.BlockSpec(memory_space=pltpu.HBM)] * 2,
        scratch_shapes=[pltpu.SemaphoreType.DMA((2,))],
        compiler_params=pltpu.CompilerParams(vmem_limit_bytes=4 * 1024 * 1024),
    )(*results)


def solution(mesh):
    counts = tuple(mesh.shape[name] for name in ("sec", "row", "col"))
    spec = P("sec", "row", "col")
    out = P(None, "sec", "row", "col")
    return jax.shard_map(
        functools.partial(local, counts), mesh=mesh, in_specs=(spec, spec),
        out_specs=(out, out), check_vma=False,
    )
```
